32 devices in a mesh: group: 2 (over x), mod: 4 (over y, core), dir: 4 (over z).
Axes of the slice: x: 2, y: 2, z: 4, core: 2. Of those that a mesh axis runs over, the one named last changes fastest.
Arguments:
- screens: float32 [8, 512, 512], P('group', 'mod'), parts along dimension 0, may hold values from -6 to 6
- footprint: int32 [8, 4, 2], P(('group', 'dir')), parts along dimension 0, may hold values from 0 to 191
- fraction: int32 [8, 4, 2], P(('group', 'dir')), parts along dimension 0, may hold values from 0 to 15
- tilt_steps: int32 [16, 2], P(('group', 'mod')), parts along dimension 0, may hold values from -64 to 64
- facet_shift: int32 [4, 2], replicated, may hold values from 80 to 160
Outputs:
- detector: float32 [8, 640, 640], P(('group', 'dir'), 'mod'), parts along dimension 0
The draws below stay inside these ranges and needn't reach their ends.
There are 2 independent parts, one for each index of `group`. The reference program is written for one: setup_inputs(seed, part) draws one part's arguments, and reference() takes and returns one part's arrays. A program takes and returns all parts, laid end to end along the dimension named above; an argument that names none is the same for every part. Nothing has to cross between parts.
All inputs are finite; a program needn't handle non-finite values.
Results may differ from the reference program's by a relative error of at most 0.0055.
Values may be sent and summed in bfloat16 or wider, within the bound.
A program may use at most 64 MiB of HBM per device.

```python
import math
import jax
import jax.numpy as jnp
from jax import lax

P_SIZE = 320
PAD = 640
S = 512
L = 4
NMOD = 8
NDIR = 4


def set_ends(values, key, low, top_value):
    extent = values.shape
    place = [jax.random.randint(jax.random.fold_in(key, axis), (), 0, extent[axis]) for axis in range(len(extent))]
    values = values.at[tuple(place)].set(low)
    longest = extent.index(max(extent))
    place[longest] = (place[longest] + 1) % extent[longest]
    return values.at[tuple(place)].set(top_value)


def steps_of(key, shape, pieces, least, largest):
    def one(dim, blocks):
        heights = jax.random.uniform(jax.random.fold_in(jax.random.fold_in(key, 6), dim), (blocks,), jnp.float32, least / len(pieces), largest / len(pieces))
        return jnp.repeat(jnp.exp(heights), shape[dim] // blocks).reshape((-1,) + (1,) * (len(shape) - dim - 1))

    gain = one(*pieces[0])
    for cut in pieces[1:]:
        gain = gain * one(*cut)
    return gain


def scatter_about(key, shape, spread, reach, split=(), kind=jnp.bfloat16):
    drawn = jax.random.normal(key, shape, jnp.float32) * spread
    if len(split) > 0:
        drawn = steps_of(key, shape, split, -0.22, 0.18) * drawn
    return jnp.clip(drawn, min=-reach, max=reach).astype(kind)


def setup_inputs(seed: int = 0, part: int = 0) -> dict:
    key_list = jax.random.split(jax.random.key(seed), 6)
    own_keys = jax.random.split(jax.random.fold_in(key_list[5], part), 6)
    return {
        "screens": scatter_about(own_keys[0], (L, S, S), 0.6, 6.0, ((1, 4),), jnp.float32),
        "footprint": set_ends(jax.random.randint(own_keys[1], (NDIR, L, 2), 0, S - P_SIZE), jax.random.fold_in(own_keys[1], 1), 0, (S - P_SIZE) - 1).astype(jnp.int32),
        "fraction": set_ends(jax.random.randint(own_keys[2], (NDIR, L, 2), 0, 16), jax.random.fold_in(own_keys[2], 1), 0, 15).astype(jnp.int32),
        "tilt_steps": set_ends(jax.random.randint(own_keys[3], (NMOD, 2), -64, 65), jax.random.fold_in(own_keys[3], 1), -64, 64).astype(jnp.int32),
        "facet_shift": set_ends(jax.random.randint(key_list[4], (4, 2), P_SIZE // 4, P_SIZE // 2 + 1), jax.random.fold_in(key_list[4], 1), P_SIZE // 4, (P_SIZE // 2 + 1) - 1).astype(jnp.int32),
    }


def as_wide(values):
    return lax.optimization_barrier(values).astype(jnp.float32)

def dft_table(count_out, count_in, direction_sign):
    out_ids = jnp.arange(count_out, dtype=jnp.int32) - count_out // 2
    in_ids = jnp.arange(count_in, dtype=jnp.int32) - count_in // 2
    turn_count = jnp.mod(out_ids[:, None] * in_ids[None, :], PAD)
    angle_map = direction_sign * 2.0 * math.pi / PAD * turn_count.astype(jnp.float32)
    normalizer = 1.0 / math.sqrt(PAD)
    return ((jnp.cos(angle_map) * normalizer).astype(jnp.bfloat16), (jnp.sin(angle_map) * normalizer).astype(jnp.bfloat16))

def left_stack(real_part, imag_part):
    return jnp.concatenate([jnp.concatenate([real_part, -imag_part], 1), jnp.concatenate([imag_part, real_part], 1)], 0)

def right_stack(real_part, imag_part):
    return jnp.concatenate([jnp.concatenate([real_part, imag_part], 1), jnp.concatenate([-imag_part, real_part], 1)], 0)

def pupil_amplitude(row_start, row_count):
    row_ids = row_start + jnp.arange(row_count, dtype=jnp.int32)
    col_ids = jnp.arange(P_SIZE, dtype=jnp.int32)
    along_y = 2 * row_ids - P_SIZE + 1
    along_x = 2 * col_ids - P_SIZE + 1
    radius_sq = along_y[:, None] * along_y[:, None] + along_x[None, :] * along_x[None, :]
    inner_edge = P_SIZE * 28 // 100 * (P_SIZE * 28 // 100)
    inside = (radius_sq <= P_SIZE * P_SIZE) & (radius_sq >= inner_edge)
    return inside.astype(jnp.float32)

def focal_mask(facet_shift):
    centred = jnp.arange(PAD, dtype=jnp.int32) - PAD // 2
    upper_half = (centred >= 0).astype(jnp.int32)
    quadrant = 2 * upper_half[:, None] + upper_half[None, :]
    shift_row = jnp.zeros((PAD, PAD), jnp.int32)
    shift_col = jnp.zeros((PAD, PAD), jnp.int32)
    for quad_idx in range(4):
        shift_row = shift_row + jnp.where(quadrant == quad_idx, facet_shift[quad_idx, 0], 0)
        shift_col = shift_col + jnp.where(quadrant == quad_idx, facet_shift[quad_idx, 1], 0)
    shift_row = shift_row * (2 * upper_half[:, None] - 1)
    shift_col = shift_col * (2 * upper_half[None, :] - 1)
    turn_count = jnp.mod(shift_row * centred[:, None] + shift_col * centred[None, :], PAD)
    angle_map = -2.0 * math.pi / PAD * turn_count.astype(jnp.float32)
    return (jnp.cos(angle_map), jnp.sin(angle_map))

def tilt_parts(tilt_table, row_ids, col_ids):
    turn_count = jnp.mod(tilt_table[:, 0, None, None] * row_ids[None, :, None] + tilt_table[:, 1, None, None] * col_ids[None, None, :], 8 * PAD)
    angle_map = 2.0 * math.pi / (8 * PAD) * turn_count.astype(jnp.float32)
    return (jnp.cos(angle_map), jnp.sin(angle_map))

def reference(screens, footprint, fraction, tilt_steps, facet_shift):
    d_re, d_im = dft_table(PAD, P_SIZE, -1.0)
    g_re, g_im = dft_table(PAD, PAD, 1.0)
    dl_big = as_wide(left_stack(d_re, d_im))
    dr_big = as_wide(right_stack(d_re.T, d_im.T))
    gl_big = as_wide(left_stack(g_re, g_im))
    gr_big = as_wide(right_stack(g_re, g_im))
    mask_cos, mask_sin = focal_mask(facet_shift)
    amplitude = pupil_amplitude(0, P_SIZE)
    row_ids = jnp.arange(P_SIZE, dtype=jnp.int32)

    def one_direction(inputs):
        offsets, fractions = inputs
        phase_map = jnp.zeros((P_SIZE, P_SIZE), jnp.float32)
        for layer_idx in range(L):
            window = lax.dynamic_slice(screens[layer_idx], (offsets[layer_idx, 0].astype(jnp.int32), offsets[layer_idx, 1].astype(jnp.int32)), (P_SIZE + 1, P_SIZE + 1))
            frac_row = fractions[layer_idx, 0].astype(jnp.float32) / 16.0
            frac_col = fractions[layer_idx, 1].astype(jnp.float32) / 16.0
            upper_rows = (1.0 - frac_col) * window[:-1, :-1] + frac_col * window[:-1, 1:]
            lower_rows = (1.0 - frac_col) * window[1:, :-1] + frac_col * window[1:, 1:]
            phase_map = phase_map + (1.0 - frac_row) * upper_rows + frac_row * lower_rows
        field_re = (amplitude * jnp.cos(phase_map)).astype(jnp.bfloat16)
        field_im = (amplitude * jnp.sin(phase_map)).astype(jnp.bfloat16)

        def one_point(running, tilt_row):
            tilt_cos, tilt_sin = tilt_parts(tilt_row[None, :], row_ids, row_ids)
            mod_re = (as_wide(field_re) * tilt_cos[0] - as_wide(field_im) * tilt_sin[0]).astype(jnp.bfloat16)
            mod_im = (as_wide(field_re) * tilt_sin[0] + as_wide(field_im) * tilt_cos[0]).astype(jnp.bfloat16)
            half_field = jnp.dot(dl_big, as_wide(jnp.concatenate([mod_re, mod_im], 0)), preferred_element_type=jnp.float32).astype(jnp.bfloat16)
            wide_half = jnp.concatenate([half_field[:PAD], half_field[PAD:]], 1)
            focal_field = jnp.dot(as_wide(wide_half), dr_big, preferred_element_type=jnp.float32)
            focal_re = focal_field[:, :PAD]
            focal_im = focal_field[:, PAD:]
            masked_re = (focal_re * mask_cos - focal_im * mask_sin).astype(jnp.bfloat16)
            masked_im = (focal_re * mask_sin + focal_im * mask_cos).astype(jnp.bfloat16)
            back_field = jnp.dot(gl_big, as_wide(jnp.concatenate([masked_re, masked_im], 0)), preferred_element_type=jnp.float32).astype(jnp.bfloat16)
            wide_back = jnp.concatenate([back_field[:PAD], back_field[PAD:]], 1)
            image_field = jnp.dot(as_wide(wide_back), gr_big, preferred_element_type=jnp.float32)
            image_re = image_field[:, :PAD]
            image_im = image_field[:, PAD:]
            return (running + image_re * image_re + image_im * image_im, None)
        running, _ = lax.scan(one_point, jnp.zeros((PAD, PAD), jnp.float32), tilt_steps)
        return running * (4.0 / NMOD)
    return lax.map(one_direction, (footprint, fraction))
```

```python
import functools
import math

import jax
import jax.numpy as jnp
import numpy as np
from jax import lax
from jax.experimental import pallas as pl
from jax.experimental.pallas import tpu as pltpu
from jax.sharding import PartitionSpec as P

P_SIZE = 320
PAD = 640
LANES = 128
RADIX = PAD // LANES
WIDE = 384
CHUNK = 32
GROUPS = P_SIZE // (2 * CHUNK)
SPLIT = 2 * LANES
MESH = pl.DeviceIdType.MESH
F32 = jnp.float32
BF16 = jnp.bfloat16
C1, C2 = math.cos(0.4 * math.pi), math.cos(0.8 * math.pi)
S1, S2 = math.sin(0.4 * math.pi), math.sin(0.8 * math.pi)


def tables():
    q, b = np.arange(LANES)[:, None], np.arange(LANES)[None, :]
    rows = []
    for s in range(RADIX):
        angle = 2.0 * np.pi / PAD * np.mod(b * (RADIX * q + s), PAD)
        re, im = np.cos(angle) / np.sqrt(PAD), np.sin(angle) / np.sqrt(PAD)
        rows.append(np.concatenate([np.concatenate([re, im], 1), np.concatenate([-im, re], 1)], 0))
    table = np.stack(rows)
    return [np.asarray(t, dtype=BF16) for t in (table, table.transpose(0, 2, 1))]


def turn_parts(steps, period):
    quarter = jnp.round(steps * (4.0 / period))
    rest = (steps - quarter * (period / 4.0)) * (2.0 * math.pi / period)
    return quadrant_parts(rest, quarter.astype(jnp.int32))


def code_parts(code):
    quarter = (code + 8192) >> 14
    rest = (code - (quarter << 14)).astype(F32) * (2.0 * math.pi / 65536)
    return quadrant_parts(rest, quarter)


def wrapped(code):
    return ((code << 16) >> 16).astype(jnp.int16)


def quadrant_parts(rest, index):
    sq = rest * rest
    sine = rest * (1.0 + sq * (-1.0 / 6 + sq * (1.0 / 120 + sq * (-1.0 / 5040 + sq * (1.0 / 362880)))))
    cosine = 1.0 + sq * (-0.5 + sq * (1.0 / 24 + sq * (-1.0 / 720 + sq * (1.0 / 40320))))
    odd = (index & 1) == 1
    cos_out = jnp.where(odd, sine, cosine)
    sin_out = jnp.where(odd, cosine, sine)
    cos_out = jnp.where(((index + 1) & 2) == 2, -cos_out, cos_out)
    sin_out = jnp.where((index & 2) == 2, -sin_out, sin_out)
    return cos_out, sin_out


def iota(shape, axis):
    return lax.broadcasted_iota(jnp.int32, shape, axis)


def dot(left, right):
    return jnp.dot(left, right, preferred_element_type=F32)


def times(a, b):
    return a[0] * b[0] - a[1] * b[1], a[0] * b[1] + a[1] * b[0]


def spread(x):
    (x0r, x0i), (x1r, x1i), (x2r, x2i) = x
    out = [None] * RADIX
    out[0] = (x0r + x1r + x2r, x0i + x1i + x2i)
    pr, pi = x0r + C1 * x1r + C2 * x2r, x0i + C1 * x1i + C2 * x2i
    qr, qi = S1 * x1r + S2 * x2r, S1 * x1i + S2 * x2i
    out[1], out[4] = (pr + qi, pi - qr), (pr - qi, pi + qr)
    pr, pi = x0r + C2 * x1r + C1 * x2r, x0i + C2 * x1i + C1 * x2i
    qr, qi = S2 * x1r - S1 * x2r, S2 * x1i - S1 * x2i
    out[2], out[3] = (pr + qi, pi - qr), (pr - qi, pi + qr)
    return out


def spread_two(x):
    (x0r, x0i), (x1r, x1i) = x
    out = [None] * RADIX
    out[0] = (x0r + x1r, x0i + x1i)
    pr, pi, qr, qi = x0r + C1 * x1r, x0i + C1 * x1i, S1 * x1r, S1 * x1i
    out[1], out[4] = (pr + qi, pi - qr), (pr - qi, pi + qr)
    pr, pi, qr, qi = x0r + C2 * x1r, x0i + C2 * x1i, S2 * x1r, S2 * x1i
    out[2], out[3] = (pr + qi, pi - qr), (pr - qi, pi + qr)
    return out


def gather_blocks(z, wanted):
    t1 = [z[1][k] + z[4][k] for k in range(2)]
    t2 = [z[2][k] + z[3][k] for k in range(2)]
    t3 = [z[1][k] - z[4][k] for k in range(2)]
    t4 = [z[2][k] - z[3][k] for k in range(2)]
    out = {0: tuple(z[0][k] + t1[k] + t2[k] for k in range(2))}
    if 1 in wanted or 4 in wanted:
        a = [z[0][k] + C1 * t1[k] + C2 * t2[k] for k in range(2)]
        b = [S1 * t3[k] + S2 * t4[k] for k in range(2)]
        out[1] = (a[0] - b[1], a[1] + b[0])
        out[4] = (a[0] + b[1], a[1] - b[0])
    if 2 in wanted or 3 in wanted:
        a = [z[0][k] + C2 * t1[k] + C1 * t2[k] for k in range(2)]
        b = [S2 * t3[k] - S1 * t4[k] for k in range(2)]
        out[2] = (a[0] - b[1], a[1] + b[0])
        out[3] = (a[0] + b[1], a[1] - b[0])
    return [out[k] for k in wanted]


def kernel(
    n, layers, band, points, skip,
    footprint_hbm, fraction_hbm, tilt_hbm, facet_hbm,
    screens_hbm, table_hbm, flipped_hbm,
    out,
    footprint, fraction, tilts, facet, screens, table, flipped,
    pick, high, low, own, snd1, rcv1, snd2, rcv2, csnd, crcv,
    col_c, col_s, base_c, base_s, step_c, step_s, mask_c, mask_s,
    half, back, acc, isnd, ircv,
    small_sem, load_sem, st, rt, s1, r1, s2, r2, s3, r3, s4, r4,
):
    m = n // 2
    total_points = points * m
    rows_out = PAD // m
    sends = GROUPS - 1 if skip else GROUPS
    me = lax.axis_index("mod")
    core = lax.rem(me, 2)
    chip = me // 2
    other = 1 - core
    partner = chip * 2 + other
    start = chip if skip else 0

    small = [
        pltpu.make_async_copy(src, dst, small_sem.at[i])
        for i, (src, dst) in enumerate(
            ((footprint_hbm, footprint), (fraction_hbm, fraction), (facet_hbm, facet), (tilt_hbm, tilts.at[0]))
        )
    ]
    loads = [
        pltpu.make_async_copy(src, dst, load_sem.at[i])
        for i, (src, dst) in enumerate(((screens_hbm, screens), (table_hbm, table), (flipped_hbm, flipped)))
    ]
    for load in small + loads:
        load.start()

    barrier = pltpu.get_barrier_semaphore()
    peers = [partner] + [lax.rem(me + 2 * k, n) for k in range(1, m)]
    for peer in peers:
        pl.semaphore_signal(barrier, inc=1, device_id={"mod": peer}, device_id_type=MESH)

    def send(src, dst, send_sem, recv_sem, target):
        return pltpu.make_async_remote_copy(
            src_ref=src, dst_ref=dst, send_sem=send_sem, recv_sem=recv_sem,
            device_id={"mod": target}, device_id_type=MESH,
        )

    for load in small[:3]:
        load.wait()
    depth = layers * band
    lane = iota((1, depth), 1)
    first_row = jnp.zeros((1, depth), jnp.int32)
    weight = jnp.zeros((1, depth), F32)
    for layer in range(layers):
        here = (lane >= layer * band) & (lane < (layer + 1) * band)
        first_row = jnp.where(here, me * band - layer * band - footprint[0, 0, layer], first_row)
        weight = jnp.where(here, fraction[0, 0, layer].astype(F32) / 16.0, weight)
    place = lane + first_row
    for which in range(2):
        owner = other if which == 0 else core
        for t in range(sends):
            row = iota((CHUNK, 1), 0) + (2 * (start + t) + owner) * CHUNK
            gap = place - row
            chosen = jnp.where(gap == 0, 1.0 - weight, jnp.where(gap == 1, weight, 0.0))
            pick[which, t * CHUNK : (t + 1) * CHUNK, :] = chosen.astype(BF16)

    loads[0].wait()
    lanes = iota((1, LANES), 1)
    for layer in range(layers):
        col = footprint[0, 1, layer]
        far = col >= LANES
        near = col & (LANES - 1)
        frac = fraction[0, 1, layer].astype(F32) / 16.0
        slabs = [screens[layer, :, j * LANES : (j + 1) * LANES] for j in range(4)]
        slabs = [jnp.where(far, slabs[min(j + 1, 3)], slabs[j]) for j in range(4)]
        turn = (LANES - near) & (LANES - 1)
        rolled = [pltpu.roll(slab, turn, 1) for slab in slabs]
        nexts = [pltpu.roll(slab, LANES - 1, 1) for slab in rolled]
        for j in range(3):
            this = jnp.where(lanes < LANES - near, rolled[j], rolled[j + 1])
            after = jnp.where(lanes < LANES - 1 - near, nexts[j], nexts[j + 1])
            value = (1.0 - frac) * this + frac * after
            value_high = value.astype(BF16)
            cut = (slice(layer * band, (layer + 1) * band), slice(j * LANES, (j + 1) * LANES))
            high[cut] = value_high
            low[cut] = (value - value_high.astype(F32)).astype(BF16)

    def partial(which):
        value = dot(pick[which], high[...]) + dot(pick[which], low[...])
        return jnp.round(value * (32768.0 / math.pi)).astype(jnp.int32)

    code = partial(0)
    for t in range(sends):
        snd1[t] = wrapped(code[t * CHUNK : (t + 1) * CHUNK])
    small[3].wait()
    pl.semaphore_wait(barrier, len(peers))
    first = []
    for t in range(sends):
        copy = send(snd1.at[t], rcv1.at[t], s1.at[t], r1.at[t], partner)
        copy.start()
        first.append(copy)
    gather = []
    for k in range(1, m):
        copy = send(tilts.at[0], tilts.at[k], st.at[k - 1], rt.at[k - 1], lax.rem(me + 2 * k, n))
        copy.start()
        gather.append(copy)
    code = partial(1)
    for t in range(sends):
        own[1 + t] = code[t * CHUNK : (t + 1) * CHUNK]
    own[0] = jnp.zeros((CHUNK, WIDE), jnp.int32)
    own[1 + sends] = jnp.zeros((CHUNK, WIDE), jnp.int32)

    def focal_mask(s):
        spot = iota((LANES, LANES), 0)
        lane = iota((LANES, LANES), 1)
        upper, right = spot < LANES // 2, lane < LANES // 2
        along_u = RADIX * spot + s - jnp.where(upper, 0, PAD)
        shift = jnp.where(
            upper,
            jnp.where(right, facet[0, 3], facet[0, 2]),
            jnp.where(right, -facet[0, 1], -facet[0, 0]),
        )
        coef = chip * rows_out - P_SIZE // 2 - shift
        row = turn_parts((coef * along_u).astype(F32), float(PAD))
        for t in range(RADIX):
            along_v = RADIX * iota((8, LANES), 1) + t
            right = iota((8, LANES), 1) < LANES // 2
            along_v = along_v - jnp.where(right, 0, PAD)
            upper = iota((8, LANES), 0) < 4
            shift = jnp.where(
                upper,
                jnp.where(right, facet[1, 3], -facet[1, 2]),
                jnp.where(right, facet[1, 1], -facet[1, 0]),
            )
            coef = -(P_SIZE // 2) - shift
            col_cos, col_sin = turn_parts((coef * along_v).astype(F32), float(PAD))
            for h in range(2):
                rows = slice(h * (LANES // 2), (h + 1) * (LANES // 2))
                pair = (col_cos[4 * h : 4 * h + 1], col_sin[4 * h : 4 * h + 1])
                re, im = times((row[0][rows], row[1][rows]), pair)
                mask_c[s, rows, t * LANES : (t + 1) * LANES] = re
                mask_s[s, rows, t * LANES : (t + 1) * LANES] = im

    focal_mask(0)
    second = []
    for t in range(sends):
        first[t].wait()
        total = own[1 + t] + rcv1[t].astype(jnp.int32)
        own[1 + t] = total
        snd2[t] = wrapped(total)
        copies = []
        for k in range(1, m):
            copy = send(
                snd2.at[t], rcv2.at[k - 1, t], s2.at[k - 1, t], r2.at[k - 1, t], lax.rem(me + 2 * k, n)
            )
            copy.start()
            copies.append(copy)
        second.append(copies)
    for s in range(1, RADIX):
        focal_mask(s)

    for load in loads[1:]:
        load.wait()
    for copy in gather:
        copy.wait()
    for k in range(m):
        for q in range(points):
            p = k * points + q
            steps = tilts[k, q : q + 1, :].astype(F32)
            down, along = steps[:, 0:1], steps[:, 1:2]
            across = along * iota((1, WIDE), 1).astype(F32)
            col_c[p : p + 1, :], col_s[p : p + 1, :] = turn_parts(across, 8.0 * PAD)
            base_c[p], base_s[p] = turn_parts(down * iota((CHUNK, LANES), 0).astype(F32), 8.0 * PAD)
            step_c[p], step_s[p] = turn_parts(
                down * (CHUNK * iota((16, LANES), 0)).astype(F32), 8.0 * PAD
            )

    def pupil_piece(code, which):
        cos_part, sin_part = code_parts(code)
        along_y = 2 * (iota((CHUNK, 1), 0) + which * CHUNK) - P_SIZE + 1
        along_x = 2 * iota((1, WIDE), 1) - P_SIZE + 1
        radius = along_y * along_y + along_x * along_x
        edge = P_SIZE * 28 // 100 * (P_SIZE * 28 // 100)
        inside = (radius <= P_SIZE * P_SIZE) & (radius >= edge)
        field = (jnp.where(inside, cos_part, 0.0), jnp.where(inside, sin_part, 0.0))
        parts = [[] for _ in range(RADIX)]
        for p in range(total_points):
            step = (step_c[p, pl.ds(which, 1), :], step_s[p, pl.ds(which, 1), :])
            blocks = []
            for j in range(3):
                cut = slice(j * LANES, (j + 1) * LANES)
                col = times(step, (col_c[p : p + 1, cut], col_s[p : p + 1, cut]))
                tilt = times((base_c[p], base_s[p]), col)
                blocks.append(times((field[0][:, cut], field[1][:, cut]), tilt))
            for s, pair in enumerate(spread(blocks)):
                parts[s].append(jnp.concatenate(pair, 1).astype(BF16))
        start_row = pl.multiple_of(which * CHUNK, CHUNK)
        for s in range(RADIX):
            wide = dot(jnp.concatenate(parts[s], 0), flipped[s])
            for p in range(total_points):
                half[p, pl.ds(start_row, CHUNK), s * SPLIT : (s + 1) * SPLIT] = wide[
                    p * CHUNK : (p + 1) * CHUNK
                ]

    shift = 1 - 2 * chip if skip else 0
    third = []
    groups = []

    def finish(step, code, group):
        csnd[step] = wrapped(code)
        copy = send(csnd.at[step], crcv.at[step], s3.at[step], r3.at[step], partner)
        copy.start()
        third.append(copy)
        groups.append(group)
        pupil_piece(code, 2 * group + core)

    def take(step):
        third[step].wait()
        pupil_piece(crcv[step].astype(jnp.int32), 2 * groups[step] + other)

    if skip:
        finish(0, own[1 + 3 * chip], chip * (GROUPS - 1))
    for t in range(sends):
        code = own[1 + t + shift]
        for k in range(1, m):
            second[t][k - 1].wait()
            code = code + rcv2[k - 1, t].astype(jnp.int32)
        step = len(third)
        finish(step, code, (1 - start if skip else 0) + t)
        if step > 0:
            take(step - 1)
    take(len(third) - 1)

    owned = rows_out // 2
    slab = acc.shape[1]
    count = owned // slab
    blocks = -(-rows_out // LANES)

    def store_back(p, s, block, pair):
        low_row, high_row = block * LANES, min((block + 1) * LANES, rows_out)
        row = low_row
        while row < high_row:
            piece = row // slab
            stop = min((piece + 1) * slab, high_row)
            where = slice(p * slab + row - piece * slab, p * slab + stop - piece * slab)
            for k in range(2):
                lanes = slice(s * SPLIT + k * LANES, s * SPLIT + (k + 1) * LANES)
                back[piece, where, lanes] = pair[k][row - low_row : stop - low_row].astype(back.dtype)
            row = stop

    def focal_tile(tile):
        mid = P_SIZE - 2 * LANES
        top, bottom = [], []
        for p, s in tile:
            def part(first, last, k):
                return half[p, first:last, s * SPLIT + k * LANES : s * SPLIT + (k + 1) * LANES]
            def pairs(first, last, count):
                return [
                    tuple(part(j * LANES + first, j * LANES + last, k) for k in range(2)) for j in range(count)
                ]
            top.append(spread(pairs(0, mid, 3)))
            bottom.append(spread_two(pairs(mid, LANES, 2)))
        z = []
        for s in range(RADIX):
            stacked = []
            for k in range(2):
                for rows in (top, bottom):
                    stacked.append(
                        jnp.concatenate([rows[i][s][k].astype(BF16) for i in range(len(tile))], 1)
                    )
            focal = dot(table[s], jnp.concatenate(stacked, 0))
            mask = tuple(
                jnp.concatenate([ref[s, :, t * LANES : (t + 1) * LANES] for _, t in tile], 1)
                for ref in (mask_c, mask_s)
            )
            masked = times((focal[:LANES], focal[LANES:]), mask)
            masked = jnp.concatenate([part.astype(BF16) for part in masked], 0)
            value = dot(flipped[s], masked)
            z.append((value[:LANES], value[LANES:]))
        for block, pair in enumerate(gather_blocks(z, list(range(blocks)))):
            for i, (p, s) in enumerate(tile):
                cut = slice(i * LANES, (i + 1) * LANES)
                store_back(p, s, block, (pair[0][:, cut], pair[1][:, cut]))

    todo = [(p, s) for p in range(total_points) for s in range(RADIX)]
    for i in range(0, len(todo), 2):
        focal_tile(todo[i : i + 2])

    def image_piece(owner, c):
        rows = back.at[owner * count + c]
        z = []
        for s in range(RADIX):
            value = dot(rows[:, s * SPLIT : (s + 1) * SPLIT].astype(BF16), table[s])
            z.append((value[:, :LANES], value[:, LANES:]))
        sums = []
        for re, im in gather_blocks(z, list(range(RADIX))):
            power = re * re + im * im
            total = power[:slab]
            for p in range(1, total_points):
                total = total + power[p * slab : (p + 1) * slab]
            sums.append(total)
        return sums

    fourth = []
    for c in range(count):
        for j, block in enumerate(image_piece(other, c)):
            isnd[c, :, j * LANES : (j + 1) * LANES] = block
        copy = send(isnd.at[c], ircv.at[c], s4.at[c], r4.at[c], partner)
        copy.start()
        fourth.append(copy)
    for c in range(count):
        for j, block in enumerate(image_piece(core, c)):
            acc[c, :, j * LANES : (j + 1) * LANES] = block
    for c in range(count):
        fourth[c].wait()
        out[0, c * slab : (c + 1) * slab, :] = acc[c] + ircv[c]


def solution(mesh):
    n = mesh.shape["mod"]
    m = n // 2
    owned = PAD // n
    slab = 80 if owned % 80 == 0 else owned
    consts = tables()

    def shards(screens, footprint, fraction, tilt_steps, facet_shift):
        layers, band, width = screens.shape
        points = tilt_steps.shape[0]
        total = points * m
        reach = 2 * CHUNK * (GROUPS - 1)
        skip = m == 2 and 2 * band <= reach and 2 * band - (width - P_SIZE) >= P_SIZE - reach
        sends = GROUPS - 1 if skip else GROUPS
        vmem = pl.BlockSpec(memory_space=pltpu.VMEM)
        hbm = pl.BlockSpec(memory_space=pltpu.HBM)
        dma = pltpu.SemaphoreType.DMA
        codes = lambda count, kind: pltpu.VMEM((count, CHUNK, WIDE), kind)
        detector = pl.pallas_call(
            functools.partial(kernel, n, layers, band, points, skip),
            out_shape=jax.ShapeDtypeStruct((1, owned, PAD), F32),
            in_specs=[hbm] * 7,
            out_specs=vmem,
            scratch_shapes=[
                pltpu.SMEM((1, 2, layers), jnp.int32),
                pltpu.SMEM((1, 2, layers), jnp.int32),
                pltpu.VMEM((m, points, 2), jnp.int32),
                pltpu.SMEM(facet_shift.shape[::-1], jnp.int32),
                pltpu.VMEM((layers, band, width), F32),
                pltpu.VMEM((RADIX, SPLIT, SPLIT), BF16),
                pltpu.VMEM((RADIX, SPLIT, SPLIT), BF16),
                pltpu.VMEM((2, sends * CHUNK, layers * band), BF16),
                pltpu.VMEM((layers * band, WIDE), BF16),
                pltpu.VMEM((layers * band, WIDE), BF16),
                codes(sends + 2, jnp.int32),
                codes(sends, jnp.int16),
                codes(sends, jnp.int16),
                codes(sends, jnp.int16),
                pltpu.VMEM((m - 1, sends, CHUNK, WIDE), jnp.int16),
                codes(GROUPS, jnp.int16),
                codes(GROUPS, jnp.int16),
                pltpu.VMEM((total, WIDE), F32),
                pltpu.VMEM((total, WIDE), F32),
                pltpu.VMEM((total, CHUNK, LANES), F32),
                pltpu.VMEM((total, CHUNK, LANES), F32),
                pltpu.VMEM((total, 16, LANES), F32),
                pltpu.VMEM((total, 16, LANES), F32),
                pltpu.VMEM((RADIX, LANES, PAD), F32),
                pltpu.VMEM((RADIX, LANES, PAD), F32),
                pltpu.VMEM((total, P_SIZE, 2 * PAD), F32),
                pltpu.VMEM((2 * owned // slab, total * slab, 2 * PAD), BF16 if slab % 16 == 0 else F32),
                pltpu.VMEM((owned // slab, slab, PAD), F32),
                pltpu.VMEM((owned // slab, slab, PAD), F32),
                pltpu.VMEM((owned // slab, slab, PAD), F32),
                dma((4,)),
                dma((3,)),
                dma((m - 1,)), dma((m - 1,)),
                dma((sends,)), dma((sends,)),
                dma((m - 1, sends)), dma((m - 1, sends)),
                dma((GROUPS,)), dma((GROUPS,)),
                dma((owned // slab,)), dma((owned // slab,)),
            ],
            compiler_params=pltpu.CompilerParams(
                collective_id=0, has_side_effects=True, vmem_limit_bytes=60 * 1024 * 1024
            ),
        )(footprint.swapaxes(1, 2), fraction.swapaxes(1, 2), tilt_steps, facet_shift.T, screens, *[jnp.asarray(t) for t in consts])
        return detector * (4.0 / (points * n))

    placed = (
        P("group", "mod", None),
        P(("group", "dir"), None, None),
        P(("group", "dir"), None, None),
        P(("group", "mod"), None),
        P(),
    )
    return jax.shard_map(
        shards,
        mesh=mesh,
        in_specs=placed,
        out_specs=P(("group", "dir"), "mod", None),
        check_vma=False,
    )
```

```python
import functools
import math

import jax
import jax.numpy as jnp
import numpy as np
from jax import lax
from jax.experimental import pallas as pl
from jax.experimental.pallas import tpu as pltpu
from jax.sharding import PartitionSpec as P

P_SIZE = 320
PAD = 640
LANES = 128
RADIX = PAD // LANES
WIDE = 384
CHUNK = 32
GROUPS = P_SIZE // (2 * CHUNK)
SPLIT = 2 * LANES
MESH = pl.DeviceIdType.MESH
F32 = jnp.float32
BF16 = jnp.bfloat16
SINE = (9.99999604e-01, -1.66665534e-01, 8.33240745e-03, -1.98087363e-04, 2.69981853e-06, -2.03660579e-08)
COSINE = (9.99999221e-01, -4.99994267e-01, 4.16598211e-02, -1.38589124e-03, 2.42043555e-05, -2.19786764e-07)
KEEP = math.sqrt(5.0) / 4.0
S1, S2 = math.sin(0.4 * math.pi), math.sin(0.8 * math.pi)


def tables():
    q, b = np.arange(LANES)[:, None], np.arange(LANES)[None, :]
    rows = []
    for s in range(RADIX):
        angle = 2.0 * np.pi / PAD * np.mod(b * (RADIX * q + s), PAD)
        re, im = np.cos(angle) / np.sqrt(PAD), np.sin(angle) / np.sqrt(PAD)
        rows.append(np.concatenate([np.concatenate([re, im], 1), np.concatenate([-im, re], 1)], 0))
    table = np.stack(rows)
    return [np.asarray(t, dtype=BF16) for t in (table, table.transpose(0, 2, 1))]


def turn_parts(steps, period):
    quarter = jnp.round(steps * (4.0 / period))
    rest = (steps - quarter * (period / 4.0)) * (2.0 * math.pi / period)
    return quadrant_parts(rest, quarter.astype(jnp.int32))


def code_parts(code):
    turn = ((code << 16) >> 16).astype(F32) * (math.pi / 32768)
    sq = turn * turn
    sine, cosine = SINE[-1] * sq + SINE[-2], COSINE[-1] * sq + COSINE[-2]
    for factor in SINE[-3::-1]:
        sine = sine * sq + factor
    for factor in COSINE[-3::-1]:
        cosine = cosine * sq + factor
    return cosine, turn * sine


def wrapped(code):
    return ((code << 16) >> 16).astype(jnp.int16)


def quadrant_parts(rest, index):
    sq = rest * rest
    sine = rest * (1.0 + sq * (-1.0 / 6 + sq * (1.0 / 120 + sq * (-1.0 / 5040 + sq * (1.0 / 362880)))))
    cosine = 1.0 + sq * (-0.5 + sq * (1.0 / 24 + sq * (-1.0 / 720 + sq * (1.0 / 40320))))
    odd = (index & 1) == 1
    cos_out = jnp.where(odd, sine, cosine)
    sin_out = jnp.where(odd, cosine, sine)
    cos_out = jnp.where(((index + 1) & 2) == 2, -cos_out, cos_out)
    sin_out = jnp.where((index & 2) == 2, -sin_out, sin_out)
    return cos_out, sin_out


def iota(shape, axis):
    return lax.broadcasted_iota(jnp.int32, shape, axis)


def dot(left, right):
    return jnp.dot(left, right, preferred_element_type=F32)


def times(a, b):
    return a[0] * b[0] - a[1] * b[1], a[0] * b[1] + a[1] * b[0]


def spread(x):
    if len(x) == 2:
        near = [(x[0][k] - 0.25 * x[1][k], KEEP * x[1][k]) for k in range(2)]
        first = [x[0][k] + x[1][k] for k in range(2)]
        q1 = [S1 * x[1][k] for k in range(2)]
        q2 = [S2 * x[1][k] for k in range(2)]
    else:
        both = [x[1][k] + x[2][k] for k in range(2)]
        near = [(x[0][k] - 0.25 * both[k], KEEP * (x[1][k] - x[2][k])) for k in range(2)]
        first = [x[0][k] + both[k] for k in range(2)]
        q1 = [S1 * x[1][k] + S2 * x[2][k] for k in range(2)]
        q2 = [S2 * x[1][k] - S1 * x[2][k] for k in range(2)]
    p1 = [w + v for w, v in near]
    p2 = [w - v for w, v in near]
    return [
        tuple(first),
        (p1[0] + q1[1], p1[1] - q1[0]),
        (p2[0] + q2[1], p2[1] - q2[0]),
        (p2[0] - q2[1], p2[1] + q2[0]),
        (p1[0] - q1[1], p1[1] + q1[0]),
    ]


def gather_blocks(z, wanted):
    t1 = [z[1][k] + z[4][k] for k in range(2)]
    t2 = [z[2][k] + z[3][k] for k in range(2)]
    t3 = [z[1][k] - z[4][k] for k in range(2)]
    t4 = [z[2][k] - z[3][k] for k in range(2)]
    both = [t1[k] + t2[k] for k in range(2)]
    near = [(z[0][k] - 0.25 * both[k], KEEP * (t1[k] - t2[k])) for k in range(2)]
    p1 = [w + v for w, v in near]
    p2 = [w - v for w, v in near]
    q1 = [S1 * t3[k] + S2 * t4[k] for k in range(2)]
    q2 = [S2 * t3[k] - S1 * t4[k] for k in range(2)]
    out = [
        tuple(z[0][k] + both[k] for k in range(2)),
        (p1[0] - q1[1], p1[1] + q1[0]),
        (p2[0] - q2[1], p2[1] + q2[0]),
        (p2[0] + q2[1], p2[1] - q2[0]),
        (p1[0] + q1[1], p1[1] - q1[0]),
    ]
    return [out[k] for k in wanted]


def kernel(
    n, layers, band, points, skip,
    footprint_hbm, fraction_hbm, tilt_hbm, facet_hbm,
    screens_hbm, table_hbm, flipped_hbm,
    out,
    footprint, fraction, tilts, facet, screens, table, flipped,
    pick, high, low, own, snd1, rcv1, snd2, rcv2, csnd, crcv,
    tilt_c, tilt_s, mask_c, mask_s,
    half, work_a, work_b, masked_a, masked_b, blocks_a, blocks_b, wide, back, acc, isnd, ircv,
    small_sem, load_sem, st, rt, s1, r1, s2, r2, s3, r3, s4, r4,
):
    m = n // 2
    total_points = points * m
    rows_out = PAD // m
    sends = GROUPS - 1 if skip else GROUPS
    me = lax.axis_index("mod")
    core = lax.rem(me, 2)
    chip = me // 2
    other = 1 - core
    partner = chip * 2 + other
    start = chip if skip else 0

    small = [
        pltpu.make_async_copy(src, dst, small_sem.at[i])
        for i, (src, dst) in enumerate(
            ((footprint_hbm, footprint), (fraction_hbm, fraction), (facet_hbm, facet), (tilt_hbm, tilts.at[0]))
        )
    ]
    loads = [
        pltpu.make_async_copy(src, dst, load_sem.at[i])
        for i, (src, dst) in enumerate(((screens_hbm, screens), (table_hbm, table), (flipped_hbm, flipped)))
    ]
    for load in small + loads:
        load.start()

    barrier = pltpu.get_barrier_semaphore()
    peers = [partner] + [lax.rem(me + 2 * k, n) for k in range(1, m)]
    for peer in peers:
        pl.semaphore_signal(barrier, inc=1, device_id={"mod": peer}, device_id_type=MESH)

    def send(src, dst, send_sem, recv_sem, target):
        return pltpu.make_async_remote_copy(
            src_ref=src, dst_ref=dst, send_sem=send_sem, recv_sem=recv_sem,
            device_id={"mod": target}, device_id_type=MESH,
        )

    for load in small[:3]:
        load.wait()
    depth = layers * band
    lane = iota((1, depth), 1)
    first_row = jnp.zeros((1, depth), jnp.int32)
    weight = jnp.zeros((1, depth), F32)
    for layer in range(layers):
        here = (lane >= layer * band) & (lane < (layer + 1) * band)
        first_row = jnp.where(here, me * band - layer * band - footprint[0, 0, layer], first_row)
        weight = jnp.where(here, fraction[0, 0, layer].astype(F32) / 16.0, weight)
    place = lane + first_row
    for which in range(2):
        owner = other if which == 0 else core
        for t in range(sends):
            row = iota((CHUNK, 1), 0) + (2 * (start + t) + owner) * CHUNK
            gap = place - row
            chosen = jnp.where(gap == 0, 1.0 - weight, jnp.where(gap == 1, weight, 0.0))
            pick[which, t * CHUNK : (t + 1) * CHUNK, :] = chosen.astype(BF16)

    def row_factor(rows, along):
        right = iota((rows, LANES), 1) < LANES // 2
        upper = iota((rows, LANES), 0) < rows // 2
        shift = jnp.where(
            upper,
            jnp.where(right, facet[0, 3], facet[0, 2]),
            jnp.where(right, -facet[0, 1], -facet[0, 0]),
        )
        return turn_parts(((chip * rows_out - P_SIZE // 2 - shift) * along).astype(F32), float(PAD))

    def col_factor(t):
        along = RADIX * iota((8, LANES), 1) + t
        right = iota((8, LANES), 1) < LANES // 2
        upper = iota((8, LANES), 0) < 4
        shift = jnp.where(
            upper,
            jnp.where(right, facet[1, 3], -facet[1, 2]),
            jnp.where(right, facet[1, 1], -facet[1, 0]),
        )
        coef = -(P_SIZE // 2) - shift
        return turn_parts((coef * (along - jnp.where(right, 0, PAD))).astype(F32), float(PAD))

    spot = iota((LANES, LANES), 0)
    row_first = row_factor(LANES, RADIX * spot - jnp.where(spot < LANES // 2, 0, PAD))
    cols = [col_factor(t) for t in range(RADIX)]

    def focal_mask(s):
        factors = [[] for _ in range(RADIX)]
        step = row_factor(8, s)
        for h in range(2):
            rows = slice(h * (LANES // 2), (h + 1) * (LANES // 2))
            row = tuple(part[rows] for part in row_first)
            if s > 0:
                row = times(row, tuple(part[4 * h : 4 * h + 1] for part in step))
            for t in range(RADIX):
                factors[t].append(times(row, tuple(part[4 * h : 4 * h + 1] for part in cols[t])))
        for v in range(RADIX):
            for h in range(2):
                rows = slice(h * (LANES // 2), (h + 1) * (LANES // 2))
                for k, ref in enumerate((mask_c, mask_s)):
                    both = [factors[(2 * v + l) % RADIX][h][k] for l in range(2)]
                    ref[v, s, rows, :] = jnp.concatenate(both, 1).astype(ref.dtype)

    for s in range(1):
        focal_mask(s)

    loads[0].wait()
    lanes = iota((1, LANES), 1)
    for layer in range(layers):
        col = footprint[0, 1, layer]
        far = col >= LANES
        near = col & (LANES - 1)
        frac = fraction[0, 1, layer].astype(F32) / 16.0
        slabs = [screens[layer, :, j * LANES : (j + 1) * LANES] for j in range(4)]
        slabs = [jnp.where(far, slabs[min(j + 1, 3)], slabs[j]) for j in range(4)]
        turn = (LANES - near) & (LANES - 1)
        rolled = [pltpu.roll(slab, turn, 1) for slab in slabs]
        nexts = [pltpu.roll(slab, LANES - 1, 1) for slab in rolled]
        for j in range(3):
            this = jnp.where(lanes < LANES - near, rolled[j], rolled[j + 1])
            after = jnp.where(lanes < LANES - 1 - near, nexts[j], nexts[j + 1])
            value = (1.0 - frac) * this + frac * after
            value_high = value.astype(BF16)
            cut = (slice(layer * band, (layer + 1) * band), slice(j * LANES, (j + 1) * LANES))
            high[cut] = value_high
            low[cut] = (value - value_high.astype(F32)).astype(BF16)

    def partial(which):
        value = dot(pick[which], high[...]) + dot(pick[which], low[...])
        return jnp.round(value * (32768.0 / math.pi)).astype(jnp.int32)

    code = partial(0)
    for t in range(sends):
        snd1[t] = wrapped(code[t * CHUNK : (t + 1) * CHUNK])
    small[3].wait()
    pl.semaphore_wait(barrier, len(peers))
    first = []
    for t in range(sends):
        copy = send(snd1.at[t], rcv1.at[t], s1.at[t], r1.at[t], partner)
        copy.start()
        first.append(copy)
    gather = []
    for k in range(1, m):
        copy = send(tilts.at[0], tilts.at[k], st.at[k - 1], rt.at[k - 1], lax.rem(me + 2 * k, n))
        copy.start()
        gather.append(copy)
    code = partial(1)
    for t in range(sends):
        own[1 + t] = code[t * CHUNK : (t + 1) * CHUNK]
    own[0] = jnp.zeros((CHUNK, WIDE), jnp.int32)
    own[1 + sends] = jnp.zeros((CHUNK, WIDE), jnp.int32)

    second = []
    for t in range(sends):
        first[t].wait()
        total = own[1 + t] + rcv1[t].astype(jnp.int32)
        own[1 + t] = total
        snd2[t] = wrapped(total)
        copies = []
        for k in range(1, m):
            copy = send(
                snd2.at[t], rcv2.at[k - 1, t], s2.at[k - 1, t], r2.at[k - 1, t], lax.rem(me + 2 * k, n)
            )
            copy.start()
            copies.append(copy)
        second.append(copies)
    for s in range(1, RADIX):
        focal_mask(s)

    for load in loads[1:]:
        load.wait()
    for copy in gather:
        copy.wait()
    bases, jumps, acrosses = [], [], []
    for k in range(m):
        for q in range(points):
            steps = tilts[k, q : q + 1, :].astype(F32)
            down, along = steps[:, 0:1], steps[:, 1:2]
            acrosses.append(turn_parts(along * iota((8, WIDE), 1).astype(F32), 8.0 * PAD))
            bases.append(turn_parts(down * iota((CHUNK, LANES), 0).astype(F32), 8.0 * PAD))
            jumps.append(turn_parts(down * (CHUNK * iota((16, LANES), 0)).astype(F32), 8.0 * PAD))
    for which in range(2 * GROUPS):
        for j in range(3):
            cut = slice(j * LANES, (j + 1) * LANES)
            along_y = 2 * (iota((CHUNK, LANES), 0) + which * CHUNK) - P_SIZE + 1
            along_x = 2 * (iota((CHUNK, LANES), 1) + j * LANES) - P_SIZE + 1
            radius = along_y * along_y + along_x * along_x
            edge = P_SIZE * 28 // 100 * (P_SIZE * 28 // 100)
            inside = (radius <= P_SIZE * P_SIZE) & (radius >= edge)
            for p in range(total_points):
                step = tuple(part[which : which + 1] for part in jumps[p])
                col = times(step, tuple(part[0:1, cut] for part in acrosses[p]))
                re, im = times(bases[p], col)
                tilt_c[p, which, :, cut] = jnp.where(inside, re, 0.0)
                tilt_s[p, which, :, cut] = jnp.where(inside, im, 0.0)

    def pupil_piece(code, which):
        field = code_parts(code)
        parts = [[] for _ in range(RADIX)]
        for p in range(total_points):
            pair = []
            for j in range(3):
                cut = slice(j * LANES, (j + 1) * LANES)
                tilt = (tilt_c[p, which, :, cut], tilt_s[p, which, :, cut])
                pair.append(times((field[0][:, cut], field[1][:, cut]), tilt))
            for s, both in enumerate(spread(pair)):
                parts[s].append(jnp.concatenate(both, 1).astype(BF16))
        start_row = pl.multiple_of(which * CHUNK, CHUNK)
        for s in range(RADIX):
            wide = dot(jnp.concatenate(parts[s], 0), flipped[s])
            for p in range(total_points):
                half[p * RADIX + s, pl.ds(start_row, CHUNK), :] = wide[
                    p * CHUNK : (p + 1) * CHUNK
                ].astype(half.dtype)

    shift = 1 - 2 * chip if skip else 0
    third = []
    groups = []

    def pass_on(step, code, group):
        csnd[step] = wrapped(code)
        copy = send(csnd.at[step], crcv.at[step], s3.at[step], r3.at[step], partner)
        copy.start()
        third.append(copy)
        groups.append(group)
        return code

    def from_partner(step):
        third[step].wait()
        return crcv[step].astype(jnp.int32)

    if skip:
        code = pass_on(0, own[1 + 3 * chip], chip * (GROUPS - 1))
        pupil_piece(code, 2 * groups[0] + core)
        pupil_piece(from_partner(0), 2 * groups[0] + other)
    for t in range(sends):
        code = own[1 + t + shift]
        for k in range(1, m):
            second[t][k - 1].wait()
            code = code + rcv2[k - 1, t].astype(jnp.int32)
        step = len(third)
        code = pass_on(step, code, (1 - start if skip else 0) + t)
        last = from_partner(step - 1) if t > 0 else None
        pupil_piece(code, 2 * groups[step] + core)
        if last is not None:
            pupil_piece(last, 2 * groups[step - 1] + other)
    step = len(third) - 1
    pupil_piece(from_partner(step), 2 * groups[step] + other)

    owned = rows_out // 2
    slab = acc.shape[1]
    count = owned // slab
    high_blocks = -(-rows_out // LANES)
    unit = 16
    units = LANES // unit

    def store_back(p, s, first, value):
        row, stop = first, min(first + unit, rows_out)
        while row < stop:
            piece = row // slab
            end = min((piece + 1) * slab, stop)
            back[s, piece, p, row - piece * slab : end - piece * slab, :] = value[row - first : end - first].astype(
                back.dtype
            )
            row = end

    tiles = total_points * RADIX // 2
    work, masked, blocks = (work_a, work_b), (masked_a, masked_b), (blocks_a, blocks_b)

    def paired(ref, s):
        cuts = [slice(k * LANES + i * unit, k * LANES + (i + 1) * unit) for i in range(units) for k in range(2)]
        return jnp.concatenate([ref[s, cut, :] for cut in cuts], 0)

    def spread_unit(t, turn, i):
        count = 3 if (2 * LANES + (i + 1) * unit) <= P_SIZE else 2

        def part(j, k):
            rows = slice(j * LANES + i * unit, j * LANES + (i + 1) * unit)
            return jnp.concatenate(
                [half[2 * t + l, rows, k * LANES : (k + 1) * LANES].astype(F32) for l in range(2)], 1
            )

        for s, pair in enumerate(spread([tuple(part(j, k) for k in range(2)) for j in range(count)])):
            for k in range(2):
                work[turn][s, k * LANES + i * unit : k * LANES + (i + 1) * unit, :] = pair[k].astype(BF16)

    def focal_block(t, turn, s):
        focal = dot(paired(table, s), work[turn][s])
        for i in range(units):
            value = tuple(focal[(2 * i + k) * unit : (2 * i + k + 1) * unit].astype(mask_c.dtype) for k in range(2))
            mask = tuple(ref[t % RADIX, s, i * unit : (i + 1) * unit, :] for ref in (mask_c, mask_s))
            for k, part in enumerate(times(value, mask)):
                masked[turn][s, k * LANES + i * unit : k * LANES + (i + 1) * unit, :] = part.astype(BF16)

    def back_block(turn, s):
        blocks[turn][s] = dot(paired(flipped, s), masked[turn][s])

    def gather_unit(t, turn, i):
        z = [
            tuple(blocks[turn][s, (2 * i + k) * unit : (2 * i + k + 1) * unit, :] for k in range(2))
            for s in range(RADIX)
        ]
        wanted = [a for a in range(high_blocks) if a * LANES + i * unit < rows_out]
        for a, pair in zip(wanted, gather_blocks(z, wanted)):
            for l in range(2):
                p, v = (2 * t + l) // RADIX, (2 * t + l) % RADIX
                cut = slice(l * LANES, (l + 1) * LANES)
                store_back(p, v, a * LANES + i * unit, jnp.concatenate([part[:, cut] for part in pair], 1))

    shares = [range((units * s) // RADIX, (units * (s + 1)) // RADIX) for s in range(RADIX)]

    def step(t, turn, spreads=True, focals=True, backs=True, gathers=True):
        for s in range(RADIX):
            if focals:
                focal_block(t, turn, s)
            if backs:
                back_block(1 - turn, s)
            for i in shares[s]:
                if spreads:
                    spread_unit(t + 1, 1 - turn, i)
                if gathers:
                    gather_unit(t - 2, turn, i)

    def two_steps(i, carry):
        step(2 * i + 3, 1)
        step(2 * i + 4, 0)
        return carry

    for i in range(units):
        spread_unit(0, 0, i)
    step(0, 0, backs=False, gathers=False)
    step(1, 1, gathers=False)
    step(2, 0)
    if tiles <= 16:
        for i in range((tiles - 4) // 2):
            two_steps(i, 0)
    else:
        lax.fori_loop(0, (tiles - 4) // 2, two_steps, 0)
    step(tiles - 1, 1, spreads=False)
    step(tiles, 0, spreads=False, focals=False)
    step(tiles + 1, 1, spreads=False, focals=False, backs=False)

    def image_block(piece, turn, s):
        rows = back[s, piece].reshape(total_points * slab, SPLIT)
        wide[turn % 2, s] = dot(rows.astype(BF16), table[s])

    def image_rows(turn, row, dst, c):
        sums = [None] * RADIX
        for p in range(total_points):
            rows = slice(p * slab + row, p * slab + row + 8)
            z = [tuple(wide[turn % 2, s, rows, k * LANES : (k + 1) * LANES] for k in range(2)) for s in range(RADIX)]
            for j, (re, im) in enumerate(gather_blocks(z, list(range(RADIX)))):
                power = re * re + im * im
                sums[j] = power if p == 0 else sums[j] + power
        for j in range(RADIX):
            dst[c, row : row + 8, j * LANES : (j + 1) * LANES] = sums[j]

    fourth = []
    pieces = [(other * count + c, isnd, c) for c in range(count)] + [(core * count + c, acc, c) for c in range(count)]
    for turn in range(len(pieces) + 1):
        for s in range(RADIX):
            if turn < len(pieces):
                image_block(pieces[turn][0], turn, s)
            if turn > 0:
                _, dst, c = pieces[turn - 1]
                rows = list(range(0, slab, 8))
                for row in rows[(len(rows) * s) // RADIX : (len(rows) * (s + 1)) // RADIX]:
                    image_rows(turn - 1, row, dst, c)
        if 0 < turn <= count:
            c = turn - 1
            copy = send(isnd.at[c], ircv.at[c], s4.at[c], r4.at[c], partner)
            copy.start()
            fourth.append(copy)
    for c in range(count):
        fourth[c].wait()
        out[0, c * slab : (c + 1) * slab, :] = acc[c] + ircv[c]


def solution(mesh):
    n = mesh.shape["mod"]
    m = n // 2
    owned = PAD // n
    slab = 80 if owned % 80 == 0 else owned
    consts = tables()

    def shards(screens, footprint, fraction, tilt_steps, facet_shift):
        layers, band, width = screens.shape
        points = tilt_steps.shape[0]
        total = points * m
        reach = 2 * CHUNK * (GROUPS - 1)
        skip = m == 2 and 2 * band <= reach and 2 * band - (width - P_SIZE) >= P_SIZE - reach
        sends = GROUPS - 1 if skip else GROUPS
        vmem = pl.BlockSpec(memory_space=pltpu.VMEM)
        hbm = pl.BlockSpec(memory_space=pltpu.HBM)
        dma = pltpu.SemaphoreType.DMA
        codes = lambda count, kind: pltpu.VMEM((count, CHUNK, WIDE), kind)
        detector = pl.pallas_call(
            functools.partial(kernel, n, layers, band, points, skip),
            out_shape=pltpu.VMEM((1, owned, PAD), F32),
            in_specs=[hbm] * 7,
            out_specs=vmem,
            scratch_shapes=[
                pltpu.SMEM((1, 2, layers), jnp.int32),
                pltpu.SMEM((1, 2, layers), jnp.int32),
                pltpu.VMEM((m, points, 2), jnp.int32),
                pltpu.SMEM(facet_shift.shape[::-1], jnp.int32),
                pltpu.VMEM((layers, band, width), F32),
                pltpu.VMEM((RADIX, SPLIT, SPLIT), BF16),
                pltpu.VMEM((RADIX, SPLIT, SPLIT), BF16),
                pltpu.VMEM((2, sends * CHUNK, layers * band), BF16),
                pltpu.VMEM((layers * band, WIDE), BF16),
                pltpu.VMEM((layers * band, WIDE), BF16),
                codes(sends + 2, jnp.int32),
                codes(sends, jnp.int16),
                codes(sends, jnp.int16),
                codes(sends, jnp.int16),
                pltpu.VMEM((m - 1, sends, CHUNK, WIDE), jnp.int16),
                codes(GROUPS, jnp.int16),
                codes(GROUPS, jnp.int16),
                pltpu.VMEM((total, 2 * GROUPS, CHUNK, WIDE), F32),
                pltpu.VMEM((total, 2 * GROUPS, CHUNK, WIDE), F32),
                pltpu.VMEM((RADIX, RADIX, LANES, SPLIT), BF16),
                pltpu.VMEM((RADIX, RADIX, LANES, SPLIT), BF16),
                pltpu.VMEM((total * RADIX, P_SIZE, SPLIT), F32 if total <= 8 else BF16),
                pltpu.VMEM((RADIX, SPLIT, SPLIT), BF16),
                pltpu.VMEM((RADIX, SPLIT, SPLIT), BF16),
                pltpu.VMEM((RADIX, SPLIT, SPLIT), BF16),
                pltpu.VMEM((RADIX, SPLIT, SPLIT), BF16),
                pltpu.VMEM((RADIX, SPLIT, SPLIT), F32),
                pltpu.VMEM((RADIX, SPLIT, SPLIT), F32),
                pltpu.VMEM((2, RADIX, total * slab, SPLIT), F32),
                pltpu.VMEM((RADIX, 2 * owned // slab, total, slab, SPLIT), BF16 if slab % 16 == 0 else F32),
                pltpu.VMEM((owned // slab, slab, PAD), F32),
                pltpu.VMEM((owned // slab, slab, PAD), F32),
                pltpu.VMEM((owned // slab, slab, PAD), F32),
                dma((4,)),
                dma((3,)),
                dma((m - 1,)), dma((m - 1,)),
                dma((sends,)), dma((sends,)),
                dma((m - 1, sends)), dma((m - 1, sends)),
                dma((GROUPS,)), dma((GROUPS,)),
                dma((owned // slab,)), dma((owned // slab,)),
            ],
            compiler_params=pltpu.CompilerParams(
                collective_id=0, has_side_effects=True, vmem_limit_bytes=60 * 1024 * 1024
            ),
        )(footprint.swapaxes(1, 2), fraction.swapaxes(1, 2), tilt_steps, facet_shift.T, screens, *[jnp.asarray(t) for t in consts])
        return detector * (4.0 / (points * n))

    placed = (
        P("group", "mod", None),
        P(("group", "dir"), None, None),
        P(("group", "dir"), None, None),
        P(("group", "mod"), None),
        P(),
    )
    return jax.shard_map(
        shards,
        mesh=mesh,
        in_specs=placed,
        out_specs=P(("group", "dir"), "mod", None),
        check_vma=False,
    )
```

```python
import functools
import math

import jax
import jax.numpy as jnp
import numpy as np
from jax import lax
from jax.experimental import pallas as pl
from jax.experimental.pallas import tpu as pltpu
from jax.sharding import PartitionSpec as P

P_SIZE = 320
PAD = 640
LANES = 128
RADIX = PAD // LANES
WIDE = 384
CHUNK = 32
FINE = 16
GROUPS = P_SIZE // (2 * CHUNK)
SPLIT = 2 * LANES
MESH = pl.DeviceIdType.MESH
F32 = jnp.float32
BF16 = jnp.bfloat16
SINE = (9.99999604e-01, -1.66665534e-01, 8.33240745e-03, -1.98087363e-04, 2.69981853e-06, -2.03660579e-08)
COSINE = (9.99999221e-01, -4.99994267e-01, 4.16598211e-02, -1.38589124e-03, 2.42043555e-05, -2.19786764e-07)
KEEP = math.sqrt(5.0) / 4.0
S1, S2 = math.sin(0.4 * math.pi), math.sin(0.8 * math.pi)


def tables():
    q, b = np.arange(LANES)[:, None], np.arange(LANES)[None, :]
    rows = []
    for s in range(RADIX):
        angle = 2.0 * np.pi / PAD * np.mod(b * (RADIX * q + s), PAD)
        re, im = np.cos(angle) / np.sqrt(PAD), np.sin(angle) / np.sqrt(PAD)
        rows.append(np.concatenate([np.concatenate([re, im], 1), np.concatenate([-im, re], 1)], 0))
    table = np.stack(rows)
    return [np.asarray(t, dtype=BF16) for t in (table, table.transpose(0, 2, 1))]


def turn_parts(steps, period):
    quarter = jnp.round(steps * (4.0 / period))
    rest = (steps - quarter * (period / 4.0)) * (2.0 * math.pi / period)
    return quadrant_parts(rest, quarter.astype(jnp.int32))


def code_parts(code):
    turn = ((code << 16) >> 16).astype(F32) * (math.pi / 32768)
    sq = turn * turn
    sine, cosine = SINE[-1] * sq + SINE[-2], COSINE[-1] * sq + COSINE[-2]
    for factor in SINE[-3::-1]:
        sine = sine * sq + factor
    for factor in COSINE[-3::-1]:
        cosine = cosine * sq + factor
    return cosine, turn * sine


def wrapped(code):
    return ((code << 16) >> 16).astype(jnp.int16)


def quadrant_parts(rest, index):
    sq = rest * rest
    sine = rest * (1.0 + sq * (-1.0 / 6 + sq * (1.0 / 120 + sq * (-1.0 / 5040 + sq * (1.0 / 362880)))))
    cosine = 1.0 + sq * (-0.5 + sq * (1.0 / 24 + sq * (-1.0 / 720 + sq * (1.0 / 40320))))
    odd = (index & 1) == 1
    cos_out = jnp.where(odd, sine, cosine)
    sin_out = jnp.where(odd, cosine, sine)
    cos_out = jnp.where(((index + 1) & 2) == 2, -cos_out, cos_out)
    sin_out = jnp.where((index & 2) == 2, -sin_out, sin_out)
    return cos_out, sin_out


def iota(shape, axis):
    return lax.broadcasted_iota(jnp.int32, shape, axis)


def dot(left, right):
    return jnp.dot(left, right, preferred_element_type=F32)


def times(a, b):
    return a[0] * b[0] - a[1] * b[1], a[0] * b[1] + a[1] * b[0]


def spread(x):
    if len(x) == 2:
        near = [(x[0][k] - 0.25 * x[1][k], KEEP * x[1][k]) for k in range(2)]
        first = [x[0][k] + x[1][k] for k in range(2)]
        q1 = [S1 * x[1][k] for k in range(2)]
        q2 = [S2 * x[1][k] for k in range(2)]
    else:
        both = [x[1][k] + x[2][k] for k in range(2)]
        near = [(x[0][k] - 0.25 * both[k], KEEP * (x[1][k] - x[2][k])) for k in range(2)]
        first = [x[0][k] + both[k] for k in range(2)]
        q1 = [S1 * x[1][k] + S2 * x[2][k] for k in range(2)]
        q2 = [S2 * x[1][k] - S1 * x[2][k] for k in range(2)]
    p1 = [w + v for w, v in near]
    p2 = [w - v for w, v in near]
    return [
        tuple(first),
        (p1[0] + q1[1], p1[1] - q1[0]),
        (p2[0] + q2[1], p2[1] - q2[0]),
        (p2[0] - q2[1], p2[1] + q2[0]),
        (p1[0] - q1[1], p1[1] + q1[0]),
    ]


def gather_blocks(z, wanted):
    t1 = [z[1][k] + z[4][k] for k in range(2)]
    t2 = [z[2][k] + z[3][k] for k in range(2)]
    t3 = [z[1][k] - z[4][k] for k in range(2)]
    t4 = [z[2][k] - z[3][k] for k in range(2)]
    both = [t1[k] + t2[k] for k in range(2)]
    near = [(z[0][k] - 0.25 * both[k], KEEP * (t1[k] - t2[k])) for k in range(2)]
    p1 = [w + v for w, v in near]
    p2 = [w - v for w, v in near]
    q1 = [S1 * t3[k] + S2 * t4[k] for k in range(2)]
    q2 = [S2 * t3[k] - S1 * t4[k] for k in range(2)]
    out = [
        tuple(z[0][k] + both[k] for k in range(2)),
        (p1[0] - q1[1], p1[1] + q1[0]),
        (p2[0] - q2[1], p2[1] + q2[0]),
        (p2[0] + q2[1], p2[1] - q2[0]),
        (p1[0] + q1[1], p1[1] - q1[0]),
    ]
    return [out[k] for k in wanted]


def kernel(
    n, layers, band, points, skip,
    footprint_hbm, fraction_hbm, tilt_hbm, facet_hbm,
    screens_hbm, table_hbm, flipped_hbm,
    out,
    footprint, fraction, tilts, facet, screens, table, flipped,
    pick, high, low, own, snd1, rcv1, snd2, rcv2, csnd, crcv,
    tilt_c, tilt_s, mask_c, mask_s,
    half, work_a, work_b, masked_a, masked_b, blocks_a, blocks_b, wide, back, acc, isnd, ircv,
    small_sem, load_sem, st, rt, s1, r1, s2, r2, s3, r3, s4, r4,
):
    m = n // 2
    total_points = points * m
    rows_out = PAD // m
    sends = GROUPS - 1 if skip else GROUPS
    me = lax.axis_index("mod")
    core = lax.rem(me, 2)
    chip = me // 2
    other = 1 - core
    partner = chip * 2 + other
    start = chip if skip else 0

    small = [
        pltpu.make_async_copy(src, dst, small_sem.at[i])
        for i, (src, dst) in enumerate(
            ((footprint_hbm, footprint), (fraction_hbm, fraction), (facet_hbm, facet), (tilt_hbm, tilts.at[0]))
        )
    ]
    loads = [
        pltpu.make_async_copy(src, dst, load_sem.at[i])
        for i, (src, dst) in enumerate(((screens_hbm, screens), (table_hbm, table), (flipped_hbm, flipped)))
    ]
    for load in small + loads:
        load.start()

    barrier = pltpu.get_barrier_semaphore()
    peers = [partner] + [lax.rem(me + 2 * k, n) for k in range(1, m)]
    for peer in peers:
        pl.semaphore_signal(barrier, inc=1, device_id={"mod": peer}, device_id_type=MESH)

    def send(src, dst, send_sem, recv_sem, target):
        return pltpu.make_async_remote_copy(
            src_ref=src, dst_ref=dst, send_sem=send_sem, recv_sem=recv_sem,
            device_id={"mod": target}, device_id_type=MESH,
        )

    for load in small[:3]:
        load.wait()
    depth = layers * band
    lane = iota((1, depth), 1)
    first_row = jnp.zeros((1, depth), jnp.int32)
    weight = jnp.zeros((1, depth), F32)
    for layer in range(layers):
        here = (lane >= layer * band) & (lane < (layer + 1) * band)
        first_row = jnp.where(here, me * band - layer * band - footprint[0, 0, layer], first_row)
        weight = jnp.where(here, fraction[0, 0, layer].astype(F32) / 16.0, weight)
    place = lane + first_row
    for which in range(2):
        owner = other if which == 0 else core
        for t in range(sends):
            row = iota((CHUNK, 1), 0) + (2 * (start + t) + owner) * CHUNK
            gap = place - row
            chosen = jnp.where(gap == 0, 1.0 - weight, jnp.where(gap == 1, weight, 0.0))
            pick[which, t * CHUNK : (t + 1) * CHUNK, :] = chosen.astype(BF16)

    def row_factor(rows, along):
        right = iota((rows, LANES), 1) < LANES // 2
        upper = iota((rows, LANES), 0) < rows // 2
        shift = jnp.where(
            upper,
            jnp.where(right, facet[0, 3], facet[0, 2]),
            jnp.where(right, -facet[0, 1], -facet[0, 0]),
        )
        return turn_parts(((chip * rows_out - P_SIZE // 2 - shift) * along).astype(F32), float(PAD))

    def col_factor(t):
        along = RADIX * iota((8, LANES), 1) + t
        right = iota((8, LANES), 1) < LANES // 2
        upper = iota((8, LANES), 0) < 4
        shift = jnp.where(
            upper,
            jnp.where(right, facet[1, 3], -facet[1, 2]),
            jnp.where(right, facet[1, 1], -facet[1, 0]),
        )
        coef = -(P_SIZE // 2) - shift
        return turn_parts((coef * (along - jnp.where(right, 0, PAD))).astype(F32), float(PAD))

    spot = iota((LANES, LANES), 0)
    row_first = row_factor(LANES, RADIX * spot - jnp.where(spot < LANES // 2, 0, PAD))
    cols = [col_factor(t) for t in range(RADIX)]

    def focal_mask(s):
        factors = [[] for _ in range(RADIX)]
        step = row_factor(8, s)
        for h in range(2):
            rows = slice(h * (LANES // 2), (h + 1) * (LANES // 2))
            row = tuple(part[rows] for part in row_first)
            if s > 0:
                row = times(row, tuple(part[4 * h : 4 * h + 1] for part in step))
            for t in range(RADIX):
                factors[t].append(times(row, tuple(part[4 * h : 4 * h + 1] for part in cols[t])))
        for v in range(RADIX):
            for h in range(2):
                rows = slice(h * (LANES // 2), (h + 1) * (LANES // 2))
                for k, ref in enumerate((mask_c, mask_s)):
                    both = [factors[(2 * v + l) % RADIX][h][k] for l in range(2)]
                    ref[v, s, rows, :] = jnp.concatenate(both, 1).astype(ref.dtype)

    for s in range(1):
        focal_mask(s)

    loads[0].wait()
    lanes = iota((1, LANES), 1)
    for layer in range(layers):
        col = footprint[0, 1, layer]
        far = col >= LANES
        near = col & (LANES - 1)
        frac = fraction[0, 1, layer].astype(F32) / 16.0
        slabs = [screens[layer, :, j * LANES : (j + 1) * LANES] for j in range(4)]
        slabs = [jnp.where(far, slabs[min(j + 1, 3)], slabs[j]) for j in range(4)]
        turn = (LANES - near) & (LANES - 1)
        rolled = [pltpu.roll(slab, turn, 1) for slab in slabs]
        nexts = [pltpu.roll(slab, LANES - 1, 1) for slab in rolled]
        for j in range(3):
            this = jnp.where(lanes < LANES - near, rolled[j], rolled[j + 1])
            after = jnp.where(lanes < LANES - 1 - near, nexts[j], nexts[j + 1])
            value = (1.0 - frac) * this + frac * after
            value_high = value.astype(BF16)
            cut = (slice(layer * band, (layer + 1) * band), slice(j * LANES, (j + 1) * LANES))
            high[cut] = value_high
            low[cut] = (value - value_high.astype(F32)).astype(BF16)

    def partial(which):
        value = dot(pick[which], high[...]) + dot(pick[which], low[...])
        return jnp.round(value * (32768.0 / math.pi)).astype(jnp.int32)

    code = partial(0)
    for t in range(sends):
        snd1[t] = wrapped(code[t * CHUNK : (t + 1) * CHUNK])
    small[3].wait()
    pl.semaphore_wait(barrier, len(peers))
    first = []
    for t in range(sends):
        copy = send(snd1.at[t], rcv1.at[t], s1.at[t], r1.at[t], partner)
        copy.start()
        first.append(copy)
    gather = []
    for k in range(1, m):
        copy = send(tilts.at[0], tilts.at[k], st.at[k - 1], rt.at[k - 1], lax.rem(me + 2 * k, n))
        copy.start()
        gather.append(copy)
    code = partial(1)
    for t in range(sends):
        own[1 + t] = code[t * CHUNK : (t + 1) * CHUNK]
    own[0] = jnp.zeros((CHUNK, WIDE), jnp.int32)
    own[1 + sends] = jnp.zeros((CHUNK, WIDE), jnp.int32)

    second = []
    for t in range(sends):
        first[t].wait()
        total = own[1 + t] + rcv1[t].astype(jnp.int32)
        own[1 + t] = total
        snd2[t] = wrapped(total)
        copies = []
        for k in range(1, m):
            copy = send(
                snd2.at[t], rcv2.at[k - 1, t], s2.at[k - 1, t], r2.at[k - 1, t], lax.rem(me + 2 * k, n)
            )
            copy.start()
            copies.append(copy)
        second.append(copies)
    for s in range(1, RADIX):
        focal_mask(s)

    for load in loads[1:]:
        load.wait()
    for copy in gather:
        copy.wait()
    bases, jumps, acrosses = [], [], []
    for k in range(m):
        for q in range(points):
            steps = tilts[k, q : q + 1, :].astype(F32)
            down, along = steps[:, 0:1], steps[:, 1:2]
            acrosses.append(turn_parts(along * iota((8, WIDE), 1).astype(F32), 8.0 * PAD))
            bases.append(turn_parts(down * iota((CHUNK, LANES), 0).astype(F32), 8.0 * PAD))
            jumps.append(turn_parts(down * (CHUNK * iota((16, LANES), 0)).astype(F32), 8.0 * PAD))
    for which in range(2 * GROUPS):
        for j in range(3):
            cut = slice(j * LANES, (j + 1) * LANES)
            along_y = 2 * (iota((CHUNK, LANES), 0) + which * CHUNK) - P_SIZE + 1
            along_x = 2 * (iota((CHUNK, LANES), 1) + j * LANES) - P_SIZE + 1
            radius = along_y * along_y + along_x * along_x
            edge = P_SIZE * 28 // 100 * (P_SIZE * 28 // 100)
            inside = (radius <= P_SIZE * P_SIZE) & (radius >= edge)
            for p in range(total_points):
                step = tuple(part[which : which + 1] for part in jumps[p])
                col = times(step, tuple(part[0:1, cut] for part in acrosses[p]))
                re, im = times(bases[p], col)
                tilt_c[p, which, :, cut] = jnp.where(inside, re, 0.0)
                tilt_s[p, which, :, cut] = jnp.where(inside, im, 0.0)

    def pupil_piece(code, which):
        parts = [[[] for _ in range(total_points)] for _ in range(RADIX)]
        cuts = [slice(j * LANES, (j + 1) * LANES) for j in range(3)]
        for first in range(0, CHUNK, 16):
            fresh = [[[] for _ in range(total_points)] for _ in range(RADIX)]
            for top in range(first, first + 16, 8):
                rows = slice(top, top + 8)
                field = [code_parts(code[rows, cut]) for cut in cuts]
                for p in range(total_points):
                    tilted = [
                        times(field[j], (tilt_c[p, which, rows, cuts[j]], tilt_s[p, which, rows, cuts[j]]))
                        for j in range(3)
                    ]
                    for s, both in enumerate(spread(tilted)):
                        fresh[s][p].append(jnp.concatenate(both, 1))
            for s in range(RADIX):
                for p in range(total_points):
                    parts[s][p].append(jnp.concatenate(fresh[s][p], 0).astype(BF16))
        start_row = pl.multiple_of(which * CHUNK, CHUNK)
        wides = [
            dot(jnp.concatenate([one for rows in parts[s] for one in rows], 0), flipped[s]) for s in range(RADIX)
        ]
        for t in range(total_points * RADIX // 2):
            for k in range(2):
                both = []
                for block in (2 * t, 2 * t + 1):
                    p, s = block // RADIX, block % RADIX
                    both.append(wides[s][p * CHUNK : (p + 1) * CHUNK, k * LANES : (k + 1) * LANES])
                half[t, k, pl.ds(start_row, CHUNK), :] = jnp.concatenate(both, 1).astype(BF16)

    shift = 1 - 2 * chip if skip else 0
    third = []
    groups = []

    def pass_on(step, code, group):
        csnd[step] = wrapped(code)
        copy = send(csnd.at[step], crcv.at[step], s3.at[step], r3.at[step], partner)
        copy.start()
        third.append(copy)
        groups.append(group)
        return code

    def from_partner(step):
        third[step].wait()
        return crcv[step].astype(jnp.int32)

    if skip:
        code = pass_on(0, own[1 + 3 * chip], chip * (GROUPS - 1))
        pupil_piece(code, 2 * groups[0] + core)
        pupil_piece(from_partner(0), 2 * groups[0] + other)
    for t in range(sends):
        code = own[1 + t + shift]
        for k in range(1, m):
            second[t][k - 1].wait()
            code = code + rcv2[k - 1, t].astype(jnp.int32)
        step = len(third)
        code = pass_on(step, code, (1 - start if skip else 0) + t)
        last = from_partner(step - 1) if t > 0 else None
        pupil_piece(code, 2 * groups[step] + core)
        if last is not None:
            pupil_piece(last, 2 * groups[step - 1] + other)
    step = len(third) - 1
    pupil_piece(from_partner(step), 2 * groups[step] + other)

    owned = rows_out // 2
    slab = acc.shape[1]
    count = owned // slab
    high_blocks = -(-rows_out // LANES)
    unit = 16
    units = LANES // unit

    def store_back(p, s, first, value):
        row, stop = first, min(first + FINE, rows_out)
        while row < stop:
            piece = row // slab
            end = min((piece + 1) * slab, stop)
            back[s, piece, p, row - piece * slab : end - piece * slab, :] = value[row - first : end - first].astype(
                back.dtype
            )
            row = end

    tiles = total_points * RADIX // 2
    work, masked, blocks = (work_a, work_b), (masked_a, masked_b), (blocks_a, blocks_b)

    def paired(ref, s):
        cuts = [slice(k * LANES + i * unit, k * LANES + (i + 1) * unit) for i in range(units) for k in range(2)]
        return jnp.concatenate([ref[s, cut, :] for cut in cuts], 0)

    def spread_unit(t, turn, i):
        count = 3 if (2 * LANES + (i + 1) * unit) <= P_SIZE else 2
        for first in range(i * unit, (i + 1) * unit, FINE):

            def part(j, k):
                return half[t, k, j * LANES + first : j * LANES + first + FINE, :]

            for s, pair in enumerate(spread([tuple(part(j, k) for k in range(2)) for j in range(count)])):
                for k in range(2):
                    work[turn][s, k * LANES + first : k * LANES + first + FINE, :] = pair[k].astype(BF16)

    def focal_block(t, turn, s):
        focal = dot(paired(table, s), work[turn][s])
        for i in range(units):
            value = tuple(focal[(2 * i + k) * unit : (2 * i + k + 1) * unit].astype(mask_c.dtype) for k in range(2))
            mask = tuple(ref[t % RADIX, s, i * unit : (i + 1) * unit, :] for ref in (mask_c, mask_s))
            for k, part in enumerate(times(value, mask)):
                masked[turn][s, k * LANES + i * unit : k * LANES + (i + 1) * unit, :] = part.astype(BF16)

    def back_block(turn, s):
        blocks[turn][s] = dot(paired(flipped, s), masked[turn][s])

    def gather_unit(t, turn, i):
        for first in range(i * unit, (i + 1) * unit, FINE):
            z = []
            for s in range(RADIX):
                starts = [2 * i * unit + k * unit + first - i * unit for k in range(2)]
                z.append(tuple(blocks[turn][s, start : start + FINE, :] for start in starts))
            wanted = [a for a in range(high_blocks) if a * LANES + first < rows_out]
            for a, pair in zip(wanted, gather_blocks(z, wanted)):
                for l in range(2):
                    p, v = (2 * t + l) // RADIX, (2 * t + l) % RADIX
                    cut = slice(l * LANES, (l + 1) * LANES)
                    store_back(p, v, a * LANES + first, jnp.concatenate([part[:, cut] for part in pair], 1))

    shares = [range((units * s) // RADIX, (units * (s + 1)) // RADIX) for s in range(RADIX)]

    def step(t, turn, spreads=True, focals=True, backs=True, gathers=True):
        for s in range(RADIX):
            if focals:
                focal_block(t, turn, s)
            if backs:
                back_block(1 - turn, s)
            for i in shares[s]:
                if spreads:
                    spread_unit(t + 1, 1 - turn, i)
                if gathers:
                    gather_unit(t - 2, turn, i)

    def two_steps(i, carry):
        step(2 * i + 3, 1)
        step(2 * i + 4, 0)
        return carry

    for i in range(units):
        spread_unit(0, 0, i)
    step(0, 0, backs=False, gathers=False)
    step(1, 1, gathers=False)
    step(2, 0)
    if tiles <= 16:
        for i in range((tiles - 4) // 2):
            two_steps(i, 0)
    else:
        lax.fori_loop(0, (tiles - 4) // 2, two_steps, 0)
    step(tiles - 1, 1, spreads=False)
    step(tiles, 0, spreads=False, focals=False)
    step(tiles + 1, 1, spreads=False, focals=False, backs=False)

    def image_block(piece, turn, s):
        rows = back[s, piece].reshape(total_points * slab, SPLIT)
        wide[turn % 2, s] = dot(rows.astype(BF16), table[s])

    def image_rows(turn, row, dst, c):
        sums = [None] * RADIX
        for p in range(total_points):
            rows = slice(p * slab + row, p * slab + row + 8)
            z = [tuple(wide[turn % 2, s, rows, k * LANES : (k + 1) * LANES] for k in range(2)) for s in range(RADIX)]
            for j, (re, im) in enumerate(gather_blocks(z, list(range(RADIX)))):
                power = re * re + im * im
                sums[j] = power if p == 0 else sums[j] + power
        for j in range(RADIX):
            dst[c, row : row + 8, j * LANES : (j + 1) * LANES] = sums[j]

    fourth = []
    pieces = [(other * count + c, isnd, c) for c in range(count)] + [(core * count + c, acc, c) for c in range(count)]
    for turn in range(len(pieces) + 1):
        for s in range(RADIX):
            if turn < len(pieces):
                image_block(pieces[turn][0], turn, s)
            if turn > 0:
                _, dst, c = pieces[turn - 1]
                rows = list(range(0, slab, 8))
                for row in rows[(len(rows) * s) // RADIX : (len(rows) * (s + 1)) // RADIX]:
                    image_rows(turn - 1, row, dst, c)
        if 0 < turn <= count:
            c = turn - 1
            copy = send(isnd.at[c], ircv.at[c], s4.at[c], r4.at[c], partner)
            copy.start()
            fourth.append(copy)
    for c in range(count):
        fourth[c].wait()
        out[0, c * slab : (c + 1) * slab, :] = acc[c] + ircv[c]


def solution(mesh):
    n = mesh.shape["mod"]
    m = n // 2
    owned = PAD // n
    slab = 80 if owned % 80 == 0 else owned
    consts = tables()

    def shards(screens, footprint, fraction, tilt_steps, facet_shift):
        layers, band, width = screens.shape
        points = tilt_steps.shape[0]
        total = points * m
        reach = 2 * CHUNK * (GROUPS - 1)
        skip = m == 2 and 2 * band <= reach and 2 * band - (width - P_SIZE) >= P_SIZE - reach
        sends = GROUPS - 1 if skip else GROUPS
        vmem = pl.BlockSpec(memory_space=pltpu.VMEM)
        hbm = pl.BlockSpec(memory_space=pltpu.HBM)
        dma = pltpu.SemaphoreType.DMA
        codes = lambda count, kind: pltpu.VMEM((count, CHUNK, WIDE), kind)
        detector = pl.pallas_call(
            functools.partial(kernel, n, layers, band, points, skip),
            out_shape=pltpu.VMEM((1, owned, PAD), F32),
            in_specs=[hbm] * 7,
            out_specs=vmem,
            scratch_shapes=[
                pltpu.SMEM((1, 2, layers), jnp.int32),
                pltpu.SMEM((1, 2, layers), jnp.int32),
                pltpu.VMEM((m, points, 2), jnp.int32),
                pltpu.SMEM(facet_shift.shape[::-1], jnp.int32),
                pltpu.VMEM((layers, band, width), F32),
                pltpu.VMEM((RADIX, SPLIT, SPLIT), BF16),
                pltpu.VMEM((RADIX, SPLIT, SPLIT), BF16),
                pltpu.VMEM((2, sends * CHUNK, layers * band), BF16),
                pltpu.VMEM((layers * band, WIDE), BF16),
                pltpu.VMEM((layers * band, WIDE), BF16),
                codes(sends + 2, jnp.int32),
                codes(sends, jnp.int16),
                codes(sends, jnp.int16),
                codes(sends, jnp.int16),
                pltpu.VMEM((m - 1, sends, CHUNK, WIDE), jnp.int16),
                codes(GROUPS, jnp.int16),
                codes(GROUPS, jnp.int16),
                pltpu.VMEM((total, 2 * GROUPS, CHUNK, WIDE), F32),
                pltpu.VMEM((total, 2 * GROUPS, CHUNK, WIDE), F32),
                pltpu.VMEM((RADIX, RADIX, LANES, SPLIT), BF16),
                pltpu.VMEM((RADIX, RADIX, LANES, SPLIT), BF16),
                pltpu.VMEM((total * RADIX // 2, 2, P_SIZE, SPLIT), BF16),
                pltpu.VMEM((RADIX, SPLIT, SPLIT), BF16),
                pltpu.VMEM((RADIX, SPLIT, SPLIT), BF16),
                pltpu.VMEM((RADIX, SPLIT, SPLIT), BF16),
                pltpu.VMEM((RADIX, SPLIT, SPLIT), BF16),
                pltpu.VMEM((RADIX, SPLIT, SPLIT), F32),
                pltpu.VMEM((RADIX, SPLIT, SPLIT), F32),
                pltpu.VMEM((2, RADIX, total * slab, SPLIT), F32),
                pltpu.VMEM((RADIX, 2 * owned // slab, total, slab, SPLIT), BF16 if slab % 16 == 0 else F32),
                pltpu.VMEM((owned // slab, slab, PAD), F32),
                pltpu.VMEM((owned // slab, slab, PAD), F32),
                pltpu.VMEM((owned // slab, slab, PAD), F32),
                dma((4,)),
                dma((3,)),
                dma((m - 1,)), dma((m - 1,)),
                dma((sends,)), dma((sends,)),
                dma((m - 1, sends)), dma((m - 1, sends)),
                dma((GROUPS,)), dma((GROUPS,)),
                dma((owned // slab,)), dma((owned // slab,)),
            ],
            compiler_params=pltpu.CompilerParams(
                collective_id=0, has_side_effects=True, vmem_limit_bytes=60 * 1024 * 1024
            ),
        )(footprint.swapaxes(1, 2), fraction.swapaxes(1, 2), tilt_steps, facet_shift.T, screens, *[jnp.asarray(t) for t in consts])
        return detector * (4.0 / (points * n))

    placed = (
        P("group", "mod", None),
        P(("group", "dir"), None, None),
        P(("group", "dir"), None, None),
        P(("group", "mod"), None),
        P(),
    )
    return jax.shard_map(
        shards,
        mesh=mesh,
        in_specs=placed,
        out_specs=P(("group", "dir"), "mod", None),
        check_vma=False,
    )
```

```python
import functools
import math

import jax
import jax.numpy as jnp
import numpy as np
from jax import lax
from jax.experimental import pallas as pl
from jax.experimental.pallas import tpu as pltpu
from jax.sharding import PartitionSpec as P

P_SIZE = 320
PAD = 640
LANES = 128
RADIX = PAD // LANES
WIDE = 384
CHUNK = 32
PACKED = CHUNK + 8
FINE = 16
GROUPS = P_SIZE // (2 * CHUNK)
SPLIT = 2 * LANES
MESH = pl.DeviceIdType.MESH
F32 = jnp.float32
BF16 = jnp.bfloat16
SINE = (9.99999604e-01, -1.66665534e-01, 8.33240745e-03, -1.98087363e-04, 2.69981853e-06, -2.03660579e-08)
COSINE = (9.99999221e-01, -4.99994267e-01, 4.16598211e-02, -1.38589124e-03, 2.42043555e-05, -2.19786764e-07)
KEEP = math.sqrt(5.0) / 4.0
S1, S2 = math.sin(0.4 * math.pi), math.sin(0.8 * math.pi)


def tables():
    q, b = np.arange(LANES)[:, None], np.arange(LANES)[None, :]
    rows = []
    for s in range(RADIX):
        angle = 2.0 * np.pi / PAD * np.mod(b * (RADIX * q + s), PAD)
        re, im = np.cos(angle) / np.sqrt(PAD), np.sin(angle) / np.sqrt(PAD)
        rows.append(np.concatenate([np.concatenate([re, im], 1), np.concatenate([-im, re], 1)], 0))
    table = np.stack(rows)
    return [np.asarray(t, dtype=BF16) for t in (table, table.transpose(0, 2, 1))]


def turn_parts(steps, period):
    quarter = jnp.round(steps * (4.0 / period))
    rest = (steps - quarter * (period / 4.0)) * (2.0 * math.pi / period)
    return quadrant_parts(rest, quarter.astype(jnp.int32))


def code_parts(code):
    turn = ((code << 16) >> 16).astype(F32) * (math.pi / 32768)
    sq = turn * turn
    sine, cosine = SINE[-1] * sq + SINE[-2], COSINE[-1] * sq + COSINE[-2]
    for factor in SINE[-3::-1]:
        sine = sine * sq + factor
    for factor in COSINE[-3::-1]:
        cosine = cosine * sq + factor
    return cosine, turn * sine


def wrapped(code):
    return ((code << 16) >> 16).astype(jnp.int16)


def quadrant_parts(rest, index):
    sq = rest * rest
    sine = rest * (1.0 + sq * (-1.0 / 6 + sq * (1.0 / 120 + sq * (-1.0 / 5040 + sq * (1.0 / 362880)))))
    cosine = 1.0 + sq * (-0.5 + sq * (1.0 / 24 + sq * (-1.0 / 720 + sq * (1.0 / 40320))))
    odd = (index & 1) == 1
    cos_out = jnp.where(odd, sine, cosine)
    sin_out = jnp.where(odd, cosine, sine)
    cos_out = jnp.where(((index + 1) & 2) == 2, -cos_out, cos_out)
    sin_out = jnp.where((index & 2) == 2, -sin_out, sin_out)
    return cos_out, sin_out


def pack_codes(code):
    low = iota((8, LANES), 1) < LANES // 2
    last = [code[k : k + 8, 2 * LANES :] for k in range(0, CHUNK, 8)]
    folded = [jnp.where(low, last[k], pltpu.roll(last[k + 1], LANES // 2, 1)) for k in (0, 2)]
    return jnp.concatenate([code[:, : 2 * LANES], jnp.concatenate(folded, 1)], 0)


def code_block(packed, top, j):
    if j < 2:
        return packed[top : top + 8, j * LANES : (j + 1) * LANES]
    k = top // 8
    block = packed[CHUNK:PACKED, (k // 2) * LANES : (k // 2 + 1) * LANES]
    return pltpu.roll(block, LANES // 2, 1) if k % 2 else block


def iota(shape, axis):
    return lax.broadcasted_iota(jnp.int32, shape, axis)


def dot(left, right):
    return jnp.dot(left, right, preferred_element_type=F32)


def times(a, b):
    return a[0] * b[0] - a[1] * b[1], a[0] * b[1] + a[1] * b[0]


def spread(x):
    if len(x) == 2:
        near = [(x[0][k] - 0.25 * x[1][k], KEEP * x[1][k]) for k in range(2)]
        first = [x[0][k] + x[1][k] for k in range(2)]
        q1 = [S1 * x[1][k] for k in range(2)]
        q2 = [S2 * x[1][k] for k in range(2)]
    else:
        both = [x[1][k] + x[2][k] for k in range(2)]
        near = [(x[0][k] - 0.25 * both[k], KEEP * (x[1][k] - x[2][k])) for k in range(2)]
        first = [x[0][k] + both[k] for k in range(2)]
        q1 = [S1 * x[1][k] + S2 * x[2][k] for k in range(2)]
        q2 = [S2 * x[1][k] - S1 * x[2][k] for k in range(2)]
    p1 = [w + v for w, v in near]
    p2 = [w - v for w, v in near]
    return [
        tuple(first),
        (p1[0] + q1[1], p1[1] - q1[0]),
        (p2[0] + q2[1], p2[1] - q2[0]),
        (p2[0] - q2[1], p2[1] + q2[0]),
        (p1[0] - q1[1], p1[1] + q1[0]),
    ]


def gather_blocks(z, wanted):
    t1 = [z[1][k] + z[4][k] for k in range(2)]
    t2 = [z[2][k] + z[3][k] for k in range(2)]
    t3 = [z[1][k] - z[4][k] for k in range(2)]
    t4 = [z[2][k] - z[3][k] for k in range(2)]
    both = [t1[k] + t2[k] for k in range(2)]
    near = [(z[0][k] - 0.25 * both[k], KEEP * (t1[k] - t2[k])) for k in range(2)]
    p1 = [w + v for w, v in near]
    p2 = [w - v for w, v in near]
    q1 = [S1 * t3[k] + S2 * t4[k] for k in range(2)]
    q2 = [S2 * t3[k] - S1 * t4[k] for k in range(2)]
    out = [
        tuple(z[0][k] + both[k] for k in range(2)),
        (p1[0] - q1[1], p1[1] + q1[0]),
        (p2[0] - q2[1], p2[1] + q2[0]),
        (p2[0] + q2[1], p2[1] - q2[0]),
        (p1[0] + q1[1], p1[1] - q1[0]),
    ]
    return [out[k] for k in wanted]


def kernel(
    n, layers, band, points, skip,
    footprint_hbm, fraction_hbm, tilt_hbm, facet_hbm,
    screens_hbm, table_hbm, flipped_hbm,
    out,
    footprint, fraction, tilts, facet, screens, table, flipped,
    pick, high, low, own, snd1, rcv1, snd2, rcv2, csnd, crcv,
    tilt_c, tilt_s, mask_c, mask_s,
    half, work_a, work_b, masked_a, masked_b, blocks_a, blocks_b, wide, back, acc, isnd, ircv,
    small_sem, load_sem, st, rt, s1, r1, s2, r2, s3, r3, s4, r4,
):
    m = n // 2
    total_points = points * m
    rows_out = PAD // m
    sends = GROUPS - 1 if skip else GROUPS
    me = lax.axis_index("mod")
    core = lax.rem(me, 2)
    chip = me // 2
    other = 1 - core
    partner = chip * 2 + other
    start = chip if skip else 0

    small = [
        pltpu.make_async_copy(src, dst, small_sem.at[i])
        for i, (src, dst) in enumerate(
            ((footprint_hbm, footprint), (fraction_hbm, fraction), (facet_hbm, facet), (tilt_hbm, tilts.at[0]))
        )
    ]
    loads = [
        pltpu.make_async_copy(src, dst, load_sem.at[i])
        for i, (src, dst) in enumerate(((screens_hbm, screens), (table_hbm, table), (flipped_hbm, flipped)))
    ]
    for load in small + loads:
        load.start()

    barrier = pltpu.get_barrier_semaphore()
    peers = [partner] + [lax.rem(me + 2 * k, n) for k in range(1, m)]
    for peer in peers:
        pl.semaphore_signal(barrier, inc=1, device_id={"mod": peer}, device_id_type=MESH)

    def send(src, dst, send_sem, recv_sem, target):
        return pltpu.make_async_remote_copy(
            src_ref=src, dst_ref=dst, send_sem=send_sem, recv_sem=recv_sem,
            device_id={"mod": target}, device_id_type=MESH,
        )

    for load in small[:3]:
        load.wait()
    depth = layers * band
    lane = iota((1, depth), 1)
    first_row = jnp.zeros((1, depth), jnp.int32)
    weight = jnp.zeros((1, depth), F32)
    for layer in range(layers):
        here = (lane >= layer * band) & (lane < (layer + 1) * band)
        first_row = jnp.where(here, me * band - layer * band - footprint[0, 0, layer], first_row)
        weight = jnp.where(here, fraction[0, 0, layer].astype(F32) / 16.0, weight)
    place = lane + first_row
    for which in range(2):
        owner = other if which == 0 else core
        for t in range(sends):
            row = iota((CHUNK, 1), 0) + (2 * (start + t) + owner) * CHUNK
            gap = place - row
            chosen = jnp.where(gap == 0, 1.0 - weight, jnp.where(gap == 1, weight, 0.0))
            pick[which, t * CHUNK : (t + 1) * CHUNK, :] = chosen.astype(BF16)

    def row_factor(rows, along):
        right = iota((rows, LANES), 1) < LANES // 2
        upper = iota((rows, LANES), 0) < rows // 2
        shift = jnp.where(
            upper,
            jnp.where(right, facet[0, 3], facet[0, 2]),
            jnp.where(right, -facet[0, 1], -facet[0, 0]),
        )
        return turn_parts(((chip * rows_out - P_SIZE // 2 - shift) * along).astype(F32), float(PAD))

    def col_factor(t):
        along = RADIX * iota((8, LANES), 1) + t
        right = iota((8, LANES), 1) < LANES // 2
        upper = iota((8, LANES), 0) < 4
        shift = jnp.where(
            upper,
            jnp.where(right, facet[1, 3], -facet[1, 2]),
            jnp.where(right, facet[1, 1], -facet[1, 0]),
        )
        coef = -(P_SIZE // 2) - shift
        return turn_parts((coef * (along - jnp.where(right, 0, PAD))).astype(F32), float(PAD))

    spot = iota((LANES, LANES), 0)
    row_first = row_factor(LANES, RADIX * spot - jnp.where(spot < LANES // 2, 0, PAD))
    cols = [col_factor(t) for t in range(RADIX)]

    def focal_mask(s):
        factors = [[] for _ in range(RADIX)]
        step = row_factor(8, s)
        for h in range(2):
            rows = slice(h * (LANES // 2), (h + 1) * (LANES // 2))
            row = tuple(part[rows] for part in row_first)
            if s > 0:
                row = times(row, tuple(part[4 * h : 4 * h + 1] for part in step))
            for t in range(RADIX):
                factors[t].append(times(row, tuple(part[4 * h : 4 * h + 1] for part in cols[t])))
        for v in range(RADIX):
            for h in range(2):
                rows = slice(h * (LANES // 2), (h + 1) * (LANES // 2))
                for k, ref in enumerate((mask_c, mask_s)):
                    both = [factors[(2 * v + l) % RADIX][h][k] for l in range(2)]
                    ref[v, s, rows, :] = jnp.concatenate(both, 1).astype(ref.dtype)

    for s in range(1):
        focal_mask(s)

    loads[0].wait()
    lanes = iota((1, LANES), 1)
    for layer in range(layers):
        col = footprint[0, 1, layer]
        far = col >= LANES
        near = col & (LANES - 1)
        frac = fraction[0, 1, layer].astype(F32) / 16.0
        slabs = [screens[layer, :, j * LANES : (j + 1) * LANES] for j in range(4)]
        slabs = [jnp.where(far, slabs[min(j + 1, 3)], slabs[j]) for j in range(4)]
        turn = (LANES - near) & (LANES - 1)
        rolled = [pltpu.roll(slab, turn, 1) for slab in slabs]
        nexts = [pltpu.roll(slab, LANES - 1, 1) for slab in rolled]
        for j in range(3):
            this = jnp.where(lanes < LANES - near, rolled[j], rolled[j + 1])
            after = jnp.where(lanes < LANES - 1 - near, nexts[j], nexts[j + 1])
            value = (1.0 - frac) * this + frac * after
            value_high = value.astype(BF16)
            cut = (slice(layer * band, (layer + 1) * band), slice(j * LANES, (j + 1) * LANES))
            high[cut] = value_high
            low[cut] = (value - value_high.astype(F32)).astype(BF16)

    def partial(which):
        value = dot(pick[which], high[...]) + dot(pick[which], low[...])
        return jnp.round(value * (32768.0 / math.pi)).astype(jnp.int32)

    code = partial(0)
    for t in range(sends):
        snd1[t] = wrapped(pack_codes(code[t * CHUNK : (t + 1) * CHUNK]))
    small[3].wait()
    pl.semaphore_wait(barrier, len(peers))
    first = []
    for t in range(sends):
        copy = send(snd1.at[t], rcv1.at[t], s1.at[t], r1.at[t], partner)
        copy.start()
        first.append(copy)
    gather = []
    for k in range(1, m):
        copy = send(tilts.at[0], tilts.at[k], st.at[k - 1], rt.at[k - 1], lax.rem(me + 2 * k, n))
        copy.start()
        gather.append(copy)
    code = partial(1)
    for t in range(sends):
        own[1 + t] = pack_codes(code[t * CHUNK : (t + 1) * CHUNK])
    own[0] = jnp.zeros((PACKED, SPLIT), jnp.int32)
    own[1 + sends] = jnp.zeros((PACKED, SPLIT), jnp.int32)

    second = []
    for t in range(sends):
        first[t].wait()
        total = own[1 + t] + rcv1[t].astype(jnp.int32)
        own[1 + t] = total
        snd2[t] = wrapped(total)
        copies = []
        for k in range(1, m):
            copy = send(
                snd2.at[t], rcv2.at[k - 1, t], s2.at[k - 1, t], r2.at[k - 1, t], lax.rem(me + 2 * k, n)
            )
            copy.start()
            copies.append(copy)
        second.append(copies)
    for s in range(1, RADIX):
        focal_mask(s)

    for load in loads[1:]:
        load.wait()
    for copy in gather:
        copy.wait()
    bases, jumps, acrosses = [], [], []
    for k in range(m):
        for q in range(points):
            steps = tilts[k, q : q + 1, :].astype(F32)
            down, along = steps[:, 0:1], steps[:, 1:2]
            acrosses.append(turn_parts(along * iota((8, WIDE), 1).astype(F32), 8.0 * PAD))
            bases.append(turn_parts(down * iota((CHUNK, LANES), 0).astype(F32), 8.0 * PAD))
            jumps.append(turn_parts(down * (CHUNK * iota((16, LANES), 0)).astype(F32), 8.0 * PAD))
    for which in range(2 * GROUPS):
        for j in range(3):
            cut = slice(j * LANES, (j + 1) * LANES)
            along_y = 2 * (iota((CHUNK, LANES), 0) + which * CHUNK) - P_SIZE + 1
            along_x = 2 * (iota((CHUNK, LANES), 1) + j * LANES) - P_SIZE + 1
            radius = along_y * along_y + along_x * along_x
            edge = P_SIZE * 28 // 100 * (P_SIZE * 28 // 100)
            inside = (radius <= P_SIZE * P_SIZE) & (radius >= edge)
            for p in range(total_points):
                step = tuple(part[which : which + 1] for part in jumps[p])
                col = times(step, tuple(part[0:1, cut] for part in acrosses[p]))
                re, im = times(bases[p], col)
                tilt_c[p, which, :, cut] = jnp.where(inside, re, 0.0)
                tilt_s[p, which, :, cut] = jnp.where(inside, im, 0.0)

    def pupil_piece(code, which):
        parts = [[[] for _ in range(total_points)] for _ in range(RADIX)]
        cuts = [slice(j * LANES, (j + 1) * LANES) for j in range(3)]
        for first in range(0, CHUNK, 16):
            fresh = [[[] for _ in range(total_points)] for _ in range(RADIX)]
            for top in range(first, first + 16, 8):
                rows = slice(top, top + 8)
                field = [code_parts(code_block(code, top, j)) for j in range(3)]
                for p in range(total_points):
                    tilted = [
                        times(field[j], (tilt_c[p, which, rows, cuts[j]], tilt_s[p, which, rows, cuts[j]]))
                        for j in range(3)
                    ]
                    for s, both in enumerate(spread(tilted)):
                        fresh[s][p].append(jnp.concatenate(both, 1))
            for s in range(RADIX):
                for p in range(total_points):
                    parts[s][p].append(jnp.concatenate(fresh[s][p], 0).astype(BF16))
        start_row = pl.multiple_of(which * CHUNK, CHUNK)
        def products():
            return finish_piece(parts, start_row)

        return products

    def finish_piece(parts, start_row):
        wides = [
            dot(jnp.concatenate([one for rows in parts[s] for one in rows], 0), flipped[s]) for s in range(RADIX)
        ]
        for t in range(total_points * RADIX // 2):
            for k in range(2):
                both = []
                for block in (2 * t, 2 * t + 1):
                    p, s = block // RADIX, block % RADIX
                    both.append(wides[s][p * CHUNK : (p + 1) * CHUNK, k * LANES : (k + 1) * LANES])
                half[t, k, pl.ds(start_row, CHUNK), :] = jnp.concatenate(both, 1).astype(BF16)

    shift = 1 - 2 * chip if skip else 0
    third = []
    groups = []

    def pass_on(step, code, group):
        csnd[step] = wrapped(code)
        copy = send(csnd.at[step], crcv.at[step], s3.at[step], r3.at[step], partner)
        copy.start()
        third.append(copy)
        groups.append(group)
        return code

    def from_partner(step):
        third[step].wait()
        return crcv[step].astype(jnp.int32)

    ready = []

    def prepare(code, which):
        ready.append(pupil_piece(code, which))

    def flush(keep):
        while len(ready) > keep:
            ready.pop(0)()

    if skip:
        code = pass_on(0, own[1 + 3 * chip], chip * (GROUPS - 1))
        prepare(code, 2 * groups[0] + core)
        last = from_partner(0)
        flush(0)
        prepare(last, 2 * groups[0] + other)
    for t in range(sends):
        code = own[1 + t + shift]
        for k in range(1, m):
            second[t][k - 1].wait()
            code = code + rcv2[k - 1, t].astype(jnp.int32)
        step = len(third)
        code = pass_on(step, code, (1 - start if skip else 0) + t)
        last = from_partner(step - 1) if t > 0 else None
        flush(0)
        prepare(code, 2 * groups[step] + core)
        if last is not None:
            prepare(last, 2 * groups[step - 1] + other)
    step = len(third) - 1
    last = from_partner(step)
    flush(0)
    prepare(last, 2 * groups[step] + other)
    flush(0)

    owned = rows_out // 2
    slab = acc.shape[1]
    count = owned // slab
    high_blocks = -(-rows_out // LANES)
    unit = 16
    units = LANES // unit

    def store_back(p, s, first, value):
        row, stop = first, min(first + FINE, rows_out)
        while row < stop:
            piece = row // slab
            end = min((piece + 1) * slab, stop)
            back[s, piece, p, row - piece * slab : end - piece * slab, :] = value[row - first : end - first].astype(
                back.dtype
            )
            row = end

    tiles = total_points * RADIX // 2
    work, masked, blocks = (work_a, work_b), (masked_a, masked_b), (blocks_a, blocks_b)

    def paired(ref, s):
        cuts = [slice(k * LANES + i * unit, k * LANES + (i + 1) * unit) for i in range(units) for k in range(2)]
        return jnp.concatenate([ref[s, cut, :] for cut in cuts], 0)

    def spread_unit(t, turn, i):
        count = 3 if (2 * LANES + (i + 1) * unit) <= P_SIZE else 2
        for first in range(i * unit, (i + 1) * unit, FINE):

            def part(j, k):
                return half[t, k, j * LANES + first : j * LANES + first + FINE, :]

            for s, pair in enumerate(spread([tuple(part(j, k) for k in range(2)) for j in range(count)])):
                for k in range(2):
                    work[turn][s, k * LANES + first : k * LANES + first + FINE, :] = pair[k].astype(BF16)

    def focal_block(t, turn, s):
        focal = dot(paired(table, s), work[turn][s])
        for i in range(units):
            value = tuple(focal[(2 * i + k) * unit : (2 * i + k + 1) * unit].astype(mask_c.dtype) for k in range(2))
            mask = tuple(ref[t % RADIX, s, i * unit : (i + 1) * unit, :] for ref in (mask_c, mask_s))
            for k, part in enumerate(times(value, mask)):
                masked[turn][s, k * LANES + i * unit : k * LANES + (i + 1) * unit, :] = part.astype(BF16)

    def back_block(turn, s):
        blocks[turn][s] = dot(paired(flipped, s), masked[turn][s])

    def gather_unit(t, turn, i):
        for first in range(i * unit, (i + 1) * unit, FINE):
            z = []
            for s in range(RADIX):
                starts = [2 * i * unit + k * unit + first - i * unit for k in range(2)]
                z.append(tuple(blocks[turn][s, start : start + FINE, :] for start in starts))
            wanted = [a for a in range(high_blocks) if a * LANES + first < rows_out]
            for a, pair in zip(wanted, gather_blocks(z, wanted)):
                for l in range(2):
                    p, v = (2 * t + l) // RADIX, (2 * t + l) % RADIX
                    cut = slice(l * LANES, (l + 1) * LANES)
                    store_back(p, v, a * LANES + first, jnp.concatenate([part[:, cut] for part in pair], 1))

    shares = [range((units * s) // RADIX, (units * (s + 1)) // RADIX) for s in range(RADIX)]

    def step(t, turn, spreads=True, focals=True, backs=True, gathers=True):
        for s in range(RADIX):
            if focals:
                focal_block(t, turn, s)
            if backs:
                back_block(1 - turn, s)
            for i in shares[s]:
                if spreads:
                    spread_unit(t + 1, 1 - turn, i)
                if gathers:
                    gather_unit(t - 2, turn, i)

    def two_steps(i, carry):
        step(2 * i + 3, 1)
        step(2 * i + 4, 0)
        return carry

    for i in range(units):
        spread_unit(0, 0, i)
    step(0, 0, backs=False, gathers=False)
    step(1, 1, gathers=False)
    step(2, 0)
    if tiles <= 16:
        for i in range((tiles - 4) // 2):
            two_steps(i, 0)
    else:
        lax.fori_loop(0, (tiles - 4) // 2, two_steps, 0)
    step(tiles - 1, 1, spreads=False)
    step(tiles, 0, spreads=False, focals=False)
    step(tiles + 1, 1, spreads=False, focals=False, backs=False)

    def image_block(piece, turn, s):
        rows = back[s, piece].reshape(total_points * slab, SPLIT)
        wide[turn % 2, s] = dot(rows.astype(BF16), table[s])

    def image_rows(turn, row, dst, c):
        sums = [None] * RADIX
        for p in range(total_points):
            rows = slice(p * slab + row, p * slab + row + 8)
            z = [tuple(wide[turn % 2, s, rows, k * LANES : (k + 1) * LANES] for k in range(2)) for s in range(RADIX)]
            for j, (re, im) in enumerate(gather_blocks(z, list(range(RADIX)))):
                power = re * re + im * im
                sums[j] = power if p == 0 else sums[j] + power
        for j in range(RADIX):
            dst[c, row : row + 8, j * LANES : (j + 1) * LANES] = sums[j].astype(dst.dtype)

    fourth = []
    pieces = [(other * count + c, isnd, c) for c in range(count)] + [(core * count + c, acc, c) for c in range(count)]
    for turn in range(len(pieces) + 1):
        for s in range(RADIX):
            if turn < len(pieces):
                image_block(pieces[turn][0], turn, s)
            if turn > 0:
                _, dst, c = pieces[turn - 1]
                rows = list(range(0, slab, 8))
                for row in rows[(len(rows) * s) // RADIX : (len(rows) * (s + 1)) // RADIX]:
                    image_rows(turn - 1, row, dst, c)
        if 0 < turn <= count:
            c = turn - 1
            copy = send(isnd.at[c], ircv.at[c], s4.at[c], r4.at[c], partner)
            copy.start()
            fourth.append(copy)
    for c in range(count):
        fourth[c].wait()
        out[0, c * slab : (c + 1) * slab, :] = acc[c] + ircv[c].astype(F32)


def solution(mesh):
    n = mesh.shape["mod"]
    m = n // 2
    owned = PAD // n
    slab = 80 if owned % 80 == 0 else owned
    consts = tables()

    def shards(screens, footprint, fraction, tilt_steps, facet_shift):
        layers, band, width = screens.shape
        points = tilt_steps.shape[0]
        total = points * m
        reach = 2 * CHUNK * (GROUPS - 1)
        skip = m == 2 and 2 * band <= reach and 2 * band - (width - P_SIZE) >= P_SIZE - reach
        sends = GROUPS - 1 if skip else GROUPS
        vmem = pl.BlockSpec(memory_space=pltpu.VMEM)
        hbm = pl.BlockSpec(memory_space=pltpu.HBM)
        dma = pltpu.SemaphoreType.DMA
        codes = lambda count, kind: pltpu.VMEM((count, PACKED, SPLIT), kind)
        detector = pl.pallas_call(
            functools.partial(kernel, n, layers, band, points, skip),
            out_shape=pltpu.VMEM((1, owned, PAD), F32),
            in_specs=[hbm] * 7,
            out_specs=vmem,
            scratch_shapes=[
                pltpu.SMEM((1, 2, layers), jnp.int32),
                pltpu.SMEM((1, 2, layers), jnp.int32),
                pltpu.VMEM((m, points, 2), jnp.int32),
                pltpu.SMEM(facet_shift.shape[::-1], jnp.int32),
                pltpu.VMEM((layers, band, width), F32),
                pltpu.VMEM((RADIX, SPLIT, SPLIT), BF16),
                pltpu.VMEM((RADIX, SPLIT, SPLIT), BF16),
                pltpu.VMEM((2, sends * CHUNK, layers * band), BF16),
                pltpu.VMEM((layers * band, WIDE), BF16),
                pltpu.VMEM((layers * band, WIDE), BF16),
                codes(sends + 2, jnp.int32),
                codes(sends, jnp.int16),
                codes(sends, jnp.int16),
                codes(sends, jnp.int16),
                pltpu.VMEM((m - 1, sends, PACKED, SPLIT), jnp.int16),
                codes(GROUPS, jnp.int16),
                codes(GROUPS, jnp.int16),
                pltpu.VMEM((total, 2 * GROUPS, CHUNK, WIDE), F32),
                pltpu.VMEM((total, 2 * GROUPS, CHUNK, WIDE), F32),
                pltpu.VMEM((RADIX, RADIX, LANES, SPLIT), BF16),
                pltpu.VMEM((RADIX, RADIX, LANES, SPLIT), BF16),
                pltpu.VMEM((total * RADIX // 2, 2, P_SIZE, SPLIT), BF16),
                pltpu.VMEM((RADIX, SPLIT, SPLIT), BF16),
                pltpu.VMEM((RADIX, SPLIT, SPLIT), BF16),
                pltpu.VMEM((RADIX, SPLIT, SPLIT), BF16),
                pltpu.VMEM((RADIX, SPLIT, SPLIT), BF16),
                pltpu.VMEM((RADIX, SPLIT, SPLIT), F32),
                pltpu.VMEM((RADIX, SPLIT, SPLIT), F32),
                pltpu.VMEM((2, RADIX, total * slab, SPLIT), F32),
                pltpu.VMEM((RADIX, 2 * owned // slab, total, slab, SPLIT), BF16 if slab % 16 == 0 else F32),
                pltpu.VMEM((owned // slab, slab, PAD), F32),
                pltpu.VMEM((owned // slab, slab, PAD), BF16),
                pltpu.VMEM((owned // slab, slab, PAD), BF16),
                dma((4,)),
                dma((3,)),
                dma((m - 1,)), dma((m - 1,)),
                dma((sends,)), dma((sends,)),
                dma((m - 1, sends)), dma((m - 1, sends)),
                dma((GROUPS,)), dma((GROUPS,)),
                dma((owned // slab,)), dma((owned // slab,)),
            ],
            compiler_params=pltpu.CompilerParams(
                collective_id=0, has_side_effects=True, vmem_limit_bytes=60 * 1024 * 1024
            ),
        )(footprint.swapaxes(1, 2), fraction.swapaxes(1, 2), tilt_steps, facet_shift.T, screens, *[jnp.asarray(t) for t in consts])
        return detector * (4.0 / (points * n))

    placed = (
        P("group", "mod", None),
        P(("group", "dir"), None, None),
        P(("group", "dir"), None, None),
        P(("group", "mod"), None),
        P(),
    )
    return jax.shard_map(
        shards,
        mesh=mesh,
        in_specs=placed,
        out_specs=P(("group", "dir"), "mod", None),
        check_vma=False,
    )
```
